128 devices in a mesh: gx: 4 (over z), gy: 16 (over y, x), lev: 2 (over core).
Axes of the slice: x: 4, y: 4, z: 4, core: 2. Of those that a mesh axis runs over, the one named last changes fastest.
Arguments:
- fine_state: float32 [3, 32, 384, 1536], P(None, 'lev', 'gy', 'gx'), may hold values from -6 to 6
- wind_field: float32 [2, 32, 384, 1536], P(None, 'lev', 'gy', 'gx'), may hold values from -4 to 4
- increment: float32 [3, 32, 96, 384], P(None, 'lev', 'gy', 'gx'), may hold values from -6 to 6
- misfit: float32 [3, 32, 96, 384], P(None, 'lev', 'gy', 'gx'), may hold values from -6 to 6
Outputs:
- fine_next: float32 [3, 32, 384, 1536], P(None, 'lev', 'gy', 'gx')
- gradient: float32 [3, 32, 96, 384], P(None, 'lev', 'gy', 'gx')
The draws below stay inside these ranges and needn't reach their ends.
All inputs are finite; a program needn't handle non-finite values.
Results may differ from the reference program's by a relative error of at most 0.000078.
Values sent between devices are 32-bit elements; how exact they have to be, the bound alone decides.
A program may use at most 64 MiB of HBM per device.

```python
import jax
import jax.numpy as jnp
from jax import lax

VARS = 3
LEVELS = 32
NY = 384
NX = 1536
CNY = 96
CNX = 384


def block_scale(key, shape, split, smallest, largest):
    gain = 1.0
    for position, parts in split:
        steps = jax.random.uniform(jax.random.fold_in(jax.random.fold_in(key, 6), position), (parts,), jnp.float32, smallest / len(split), largest / len(split))
        gain = gain * jnp.repeat(jnp.exp(steps), shape[position] // parts).reshape((-1,) + (1,) * (len(shape) - 1 - position))
    return gain


def scatter_about(rng, extent, scale, limit, split=(), dtype=jnp.bfloat16):
    drawn = jax.random.normal(rng, extent, jnp.float32) * scale
    if len(split) > 0:
        drawn = block_scale(rng, extent, split, -0.22, 0.18) * drawn
    return jnp.clip(drawn, min=-limit, max=limit).astype(dtype)


def setup_inputs(seed: int = 0) -> dict:
    streams_of = jax.random.split(jax.random.key(seed), 5)
    return {
        "fine_state": scatter_about(streams_of[0], (VARS, LEVELS, NY, NX), 1.0, 6.0, ((1, 2), (2, 16), (3, 4)), jnp.float32),
        "wind_field": scatter_about(streams_of[1], (2, LEVELS, NY, NX), 1.0, 4.0, ((1, 2), (2, 16), (3, 4)), jnp.float32),
        "increment": scatter_about(streams_of[2], (VARS, LEVELS, CNY, CNX), 1.0, 6.0, ((1, 2), (2, 16), (3, 4)), jnp.float32),
        "misfit": scatter_about(streams_of[3], (VARS, LEVELS, CNY, CNX), 1.0, 6.0, ((1, 2), (2, 16), (3, 4)), jnp.float32),
    }


advect = 0.25
vertical_mix = 0.1
damping = 0.3
descent = 0.5


def mixing():
    return jnp.array([0.05, 0.1, 0.2], jnp.float32).reshape(3, 1, 1, 1)


def pad_all(values):
    leading = [(0, 0)] * (values.ndim - 3)
    padded = jnp.pad(values, leading + [(1, 1), (1, 1), (0, 0)])
    return jnp.concatenate([padded[..., -1:], padded, padded[..., :1]], axis=-1)


def laplace_terms(padded):
    center = padded[:, 1:-1, 1:-1, 1:-1]
    planar = padded[:, 1:-1, 1:-1, 2:] + padded[:, 1:-1, 1:-1, :-2] + padded[:, 1:-1, 2:, 1:-1] + padded[:, 1:-1, :-2, 1:-1] - 4.0 * center
    column = padded[:, 2:, 1:-1, 1:-1] + padded[:, :-2, 1:-1, 1:-1] - 2.0 * center
    return center, mixing() * planar + vertical_mix * column


def forward_linear(padded, wind_center):
    center, spread = laplace_terms(padded)
    along_x = 0.5 * (padded[:, 1:-1, 1:-1, 2:] - padded[:, 1:-1, 1:-1, :-2])
    along_y = 0.5 * (padded[:, 1:-1, 2:, 1:-1] - padded[:, 1:-1, :-2, 1:-1])
    return center - advect * (wind_center[0] * along_x + wind_center[1] * along_y) + spread


def adjoint_linear(padded, wind_pad):
    center, spread = laplace_terms(padded)
    flux_x = wind_pad[0] * padded
    flux_y = wind_pad[1] * padded
    along_x = 0.5 * (flux_x[:, 1:-1, 1:-1, 2:] - flux_x[:, 1:-1, 1:-1, :-2])
    along_y = 0.5 * (flux_y[:, 1:-1, 2:, 1:-1] - flux_y[:, 1:-1, :-2, 1:-1])
    return center + advect * (along_x + along_y) + spread


def slope(state):
    squashed = jnp.tanh(state)
    return damping * (1.0 - squashed * squashed)


def restrict(values):
    dims_now = values.shape
    blocks = values.reshape(dims_now[0], dims_now[1], dims_now[2] // 4, 4, dims_now[3] // 4, 4)
    return jnp.mean(blocks, axis=(3, 5))


def coarse_chain(extend, cstate, cwinds, increment, misfit):
    variables = cstate.shape[0]
    stacked = extend(jnp.concatenate([cwinds, cstate, increment], axis=0))
    wind_pad = stacked[:2]
    trajectory = forward_linear(stacked[2:2 + variables], cwinds) - damping * jnp.tanh(cstate)
    delta_one = forward_linear(stacked[2 + variables:], cwinds) - slope(cstate) * increment
    delta_two = forward_linear(extend(delta_one), cwinds) - slope(trajectory) * delta_one
    residual = delta_two - misfit
    adjoint_one = adjoint_linear(extend(residual), wind_pad) - slope(trajectory) * residual
    adjoint_zero = adjoint_linear(extend(adjoint_one), wind_pad) - slope(cstate) * adjoint_one
    gradient = increment + adjoint_zero
    return gradient, increment - descent * gradient


def prolong(padded, axis):
    number = padded.shape[axis] - 2
    left = lax.slice_in_dim(padded, 0, number, axis=axis)
    middle = lax.slice_in_dim(padded, 1, number + 1, axis=axis)
    right = lax.slice_in_dim(padded, 2, number + 2, axis=axis)
    pieces = [0.375 * left + 0.625 * middle, 0.125 * left + 0.875 * middle,
              0.875 * middle + 0.125 * right, 0.625 * middle + 0.375 * right]
    joined = jnp.stack(pieces, axis=axis + 1)
    target = list(padded.shape)
    target[axis] = 4 * number
    return joined.reshape(target)


def reference(fine_state, wind_field, increment, misfit):
    cstate = restrict(fine_state)
    cwinds = restrict(wind_field)
    gradient, updated = coarse_chain(pad_all, cstate, cwinds, increment, misfit)
    widened = pad_all(updated)[:, 1:-1]
    fine_increment = prolong(prolong(widened, 3), 2)
    fine_new = fine_state + fine_increment
    fine_next = forward_linear(pad_all(fine_new), wind_field) - damping * jnp.tanh(fine_new)
    return fine_next, gradient
```

```python
import functools

import jax
import jax.numpy as jnp
from jax import lax
from jax.experimental import pallas as pl
from jax.experimental.pallas import tpu as pltpu
from jax.sharding import PartitionSpec as P

MESH = pl.DeviceIdType.MESH
F32 = jnp.float32
BF16 = jnp.bfloat16
ANY = pl.BlockSpec(memory_space=pl.ANY)

MIX = (0.05, 0.1, 0.2)
VARS, LEVS, ROWS, COLS = 3, 16, 6, 96
FROWS, FCOLS = 24, 384
NGX, NGY = 4, 16

DEPTH = (4, 4, 4, 4, 4, 5, 5, 5, 3, 3, 3)
FIELDS = len(DEPTH)


def segments_row():
    place, at = {}, 0
    for f in range(FIELDS):
        place[f] = (at, DEPTH[f])
        at += DEPTH[f]
    return place


def segments_corner():
    place, at = {}, 0
    for f in range(FIELDS):
        for k in range(1, DEPTH[f] + 1):
            place[f, k] = (at, DEPTH[f] + 1 - k)
            at += DEPTH[f] + 1 - k
    return place


SEG_ROW = segments_row()
SEG_CORNER = segments_corner()


def split_dot(x, table):
    high = x.astype(BF16)
    low = (x - high.astype(F32)).astype(BF16)
    return jnp.dot(high, table, preferred_element_type=F32) + jnp.dot(
        low, table, preferred_element_type=F32
    )


def exchange_kernel(
    fine, wind, inc, mis,
    e_cw, e_im, xm, fy, fx, fl,
    fs, im_v, half, cu, xs, fys, fxs, table, load_sem, local_sem, send_sem, recv_sem,
):
    gx, gy, lev = lax.axis_index("gx"), lax.axis_index("gy"), lax.axis_index("lev")
    gxs = (lax.rem(gx + 1, NGX), lax.rem(gx + NGX - 1, NGX))
    gys = (lax.rem(gy + 1, NGY), lax.rem(gy + NGY - 1, NGY))
    partner = (gx, gy, 1 - lev)
    near = [(gx, gys[0], lev), (gx, gys[1], lev), (gxs[0], gy, lev), (gxs[1], gy, lev)]
    near += [(gxs[h], gys[s], lev) for h in range(2) for s in range(2)] + [partner]

    barrier = pltpu.get_barrier_semaphore()
    for device in near:
        pl.semaphore_signal(barrier, inc=1, device_id=device, device_id_type=MESH)

    loads = []
    for f in range(VARS):
        loads.append(pltpu.make_async_copy(fine.at[f], fs.at[f], load_sem.at[f]))
    for f in range(2):
        loads.append(pltpu.make_async_copy(wind.at[f], fs.at[3 + f], load_sem.at[3 + f]))
    loads.append(pltpu.make_async_copy(inc, im_v.at[0:3], load_sem.at[5]))
    loads.append(pltpu.make_async_copy(mis, im_v.at[3:6], load_sem.at[6]))
    for copy in loads:
        copy.start()

    source = lax.broadcasted_iota(jnp.int32, (FCOLS, 128), 0) // 4
    target = lax.broadcasted_iota(jnp.int32, (FCOLS, 128), 1)
    table[...] = jnp.where(source == target, 0.0625, 0.0).astype(BF16)

    pl.semaphore_wait(barrier, len(near))

    started = []

    def send(src, dst, device):
        i = len(started)
        copy = pltpu.make_async_remote_copy(
            src_ref=src, dst_ref=dst, send_sem=send_sem.at[i], recv_sem=recv_sem.at[i],
            device_id=device, device_id_type=MESH,
        )
        copy.start()
        started.append(copy)
        return copy

    low_high = lambda d, s: (slice(ROWS - d, ROWS) if s == 0 else slice(0, d))
    lands = lambda d, s: (slice(5 - d, 5) if s == 0 else slice(11, 11 + d))
    tile = pl.ds(pl.multiple_of((1 - lev) * 8, 8), 8)

    y_inc = [
        send(inc.at[:, low_high(5, s)], e_im.at[0:3, lands(5, s), 0:16, :], near[s])
        for s in range(2)
    ]
    y_mis = [
        send(mis.at[:, low_high(3, s)], e_im.at[3:6, lands(3, s), 0:16, :], near[s])
        for s in range(2)
    ]
    own = [
        send(inc.at[:, :, tile, :], e_im.at[0:3, 5:11, 16:24, :], partner),
        send(mis.at[:, :, tile, :], e_im.at[3:6, 5:11, 16:24, :], partner),
    ]

    def coarsen(f):
        loads[f].wait()
        block = fs[f].reshape(LEVS * FROWS, FCOLS)
        half[...] = split_dot(block, table[...])
        for j in range(ROWS):
            total = half[pl.ds(4 * j, LEVS, stride=FROWS), :]
            for a in range(1, 4):
                total += half[pl.ds(4 * j + a, LEVS, stride=FROWS), :]
            cu[f, j] = total

    for f in range(5):
        coarsen(f)
    y_cw = [
        send(cu.at[:, low_high(4, s)], e_cw.at[:, lands(4, s), 0:16, :], near[s])
        for s in range(2)
    ]
    local = pltpu.make_async_copy(cu, e_cw.at[:, 5:11, 0:16, :], local_sem)
    local.start()
    own.append(send(cu.at[:, :, tile, :], e_cw.at[:, 5:11, 16:24, :], partner))
    edge = 15 * (1 - lev)
    own.append(send(fs.at[0:3, edge], fl, partner))

    loads[5].wait()
    loads[6].wait()
    lane = lax.broadcasted_iota(jnp.int32, (LEVS, 128), 1)

    def unit(f, j):
        if f < 5:
            return cu[f, j]
        return jnp.concatenate([im_v[f - 5, j], jnp.zeros((LEVS, 128 - COLS), F32)], axis=1)

    def packed(out, value, h, at, width):
        first = COLS - width if h == 0 else 0
        moved = pltpu.roll(value, (at - first) % 128, 1)
        return jnp.where(jnp.logical_and(lane >= at, lane < at + width), moved, out)

    zero = jnp.zeros((LEVS, 128), F32)
    for h in range(2):
        for s in range(2):
            out = zero
            for (f, k), (at, width) in SEG_CORNER.items():
                out = packed(out, unit(f, ROWS - k if s == 0 else k - 1), h, at, width)
            xs[h, 6 + s] = out
        for j in range(ROWS):
            out = zero
            for f, (at, width) in SEG_ROW.items():
                out = packed(out, unit(f, j), h, at, width)
            xs[h, j] = out
    corner = [
        [
            send(xs.at[h, 6 + s], xm.at[h, 6 + s, 0:16, :], (gxs[h], gys[s], lev))
            for s in range(2)
        ]
        for h in range(2)
    ]
    x_row = [send(xs.at[h, 0:6], xm.at[h, 0:6, 0:16, :], near[2 + h]) for h in range(2)]

    for v in range(VARS):
        for l in range(LEVS):
            fys[0, v, l : l + 1, :] = fs[v, l, FROWS - 1 : FROWS, :]
            fys[1, v, l : l + 1, :] = fs[v, l, 0:1, :]
    y_fine = [send(fys.at[s], fy.at[s], near[s]) for s in range(2)]
    lane8 = lax.broadcasted_iota(jnp.int32, (8, 128), 1)
    for v in range(VARS):
        outs = [jnp.zeros((8, 128), F32)] * 2
        for l in range(LEVS):
            for t in range(3):
                n = 3 * l + t
                first = pltpu.roll(fs[v, l, 8 * t : 8 * t + 8, 0:128], n, 1)
                last = pltpu.roll(fs[v, l, 8 * t : 8 * t + 8, 256:384], (n + 1) % 128, 1)
                outs[0] = jnp.where(lane8 == n, last, outs[0])
                outs[1] = jnp.where(lane8 == n, first, outs[1])
        fxs[0, v] = outs[0]
        fxs[1, v] = outs[1]
    x_fine = [send(fxs.at[h], fx.at[h], near[2 + h]) for h in range(2)]

    relays = []
    for s in range(2):
        y_inc[s].wait_recv()
        rows = lands(5, s)
        relays.append(
            send(e_im.at[0:3, rows, tile, :], e_im.at[0:3, rows, 16:24, :], partner)
        )
    for s in range(2):
        y_mis[s].wait_recv()
        rows = lands(3, s)
        relays.append(
            send(e_im.at[3:6, rows, tile, :], e_im.at[3:6, rows, 16:24, :], partner)
        )
    for s in range(2):
        y_cw[s].wait_recv()
        rows = lands(4, s)
        relays.append(send(e_cw.at[:, rows, tile, :], e_cw.at[:, rows, 16:24, :], partner))
    for h in range(2):
        for s in range(2):
            corner[h][s].wait_recv()
        x_row[h].wait_recv()
        relays.append(send(xm.at[h, :, tile, :], xm.at[h, :, 16:24, :], partner))
    for copy in y_fine + x_fine + own + relays:
        copy.wait_recv()
    local.wait()
    for copy in started:
        copy.wait_send()


COPIES = 28


def exchange(fine, wind, inc, mis):
    return pl.pallas_call(
        exchange_kernel,
        out_shape=(
            jax.ShapeDtypeStruct((5, 16, 24, 128), F32),
            jax.ShapeDtypeStruct((6, 16, 24, COLS), F32),
            jax.ShapeDtypeStruct((2, 8, 24, 128), F32),
            jax.ShapeDtypeStruct((2, VARS, LEVS, FCOLS), F32),
            jax.ShapeDtypeStruct((2, VARS, 8, 128), F32),
            jax.ShapeDtypeStruct((VARS, FROWS, FCOLS), F32),
        ),
        in_specs=[ANY] * 4,
        out_specs=(ANY,) * 6,
        scratch_shapes=[
            pltpu.VMEM((5, LEVS, FROWS, FCOLS), F32),
            pltpu.VMEM((6, ROWS, LEVS, COLS), F32),
            pltpu.VMEM((LEVS * FROWS, 128), F32),
            pltpu.VMEM((5, ROWS, LEVS, 128), F32),
            pltpu.VMEM((2, 8, LEVS, 128), F32),
            pltpu.VMEM((2, VARS, LEVS, FCOLS), F32),
            pltpu.VMEM((2, VARS, 8, 128), F32),
            pltpu.VMEM((FCOLS, 128), BF16),
            pltpu.SemaphoreType.DMA((7,)),
            pltpu.SemaphoreType.DMA,
            pltpu.SemaphoreType.DMA((COPIES,)),
            pltpu.SemaphoreType.DMA((COPIES,)),
        ],
        compiler_params=pltpu.CompilerParams(collective_id=0, has_side_effects=True),
        name="exchange",
    )(fine, wind, inc, mis)


def solve_kernel(
    fine, wind, inc, mis, e_cw, e_im, xm, fy, fx, fl,
    fine_next, gradient,
    cw, im, xv, fyv, fxv, fn, wf, q, st, sc, d1, res, a1, up, vr, lhs, fi, table, grad, out,
    sem, out_sem,
):
    gy, lev = lax.axis_index("gy"), lax.axis_index("lev")
    other = 17 * (1 - lev)
    empty = 17 * lev

    copies = [
        pltpu.make_async_copy(e_cw, cw, sem.at[0]),
        pltpu.make_async_copy(e_im, im, sem.at[1]),
        pltpu.make_async_copy(xm, xv, sem.at[2]),
    ]
    late = [
        pltpu.make_async_copy(fy, fyv, sem.at[3]),
        pltpu.make_async_copy(fx, fxv, sem.at[4]),
        pltpu.make_async_copy(wind, wf, sem.at[5]),
    ]
    for v in range(VARS):
        late.append(
            pltpu.make_async_copy(fine.at[v], fn.at[v, 1:17, 0:24, 0:FCOLS], sem.at[6 + v])
        )
    late.append(pltpu.make_async_copy(fl, fn.at[:, other, 0:24, 0:FCOLS], sem.at[9]))
    own = [
        pltpu.make_async_copy(inc, im.at[0:3, 5:11, 0:16, :], sem.at[10]),
        pltpu.make_async_copy(mis, im.at[3:6, 5:11, 0:16, :], sem.at[11]),
    ]
    for copy in copies:
        copy.start()
    for copy in late:
        copy.start()

    source = lax.broadcasted_iota(jnp.int32, (128, 512), 0)
    target = lax.broadcasted_iota(jnp.int32, (128, 512), 1)
    target = jnp.where(target < 448, target, target - 512)
    scaled = 4 * target + 10
    beneath = lax.shift_right_arithmetic(scaled, 4)
    fraction = jnp.bitwise_and(scaled, 15).astype(F32) * 0.0625
    weights = jnp.where(source == jnp.bitwise_and(beneath - 1, 127), 1.0 - fraction, 0.0)
    weights += jnp.where(source == jnp.bitwise_and(beneath, 127), fraction, 0.0)
    table[...] = weights.astype(BF16)
    for v in range(VARS):
        fn[v, empty, 0:24, 0:FCOLS] = jnp.zeros((24, FCOLS), F32)
        vr[v, pl.ds(25 * 24, 6 * 24), :] = jnp.zeros((6 * 24, 128), F32)

    lane = lax.broadcasted_iota(jnp.int32, (24, 128), 1)
    level = lax.broadcasted_iota(jnp.int32, (24, 128), 0)
    top = jnp.where(lev == 1, 15, 24)
    bottom = jnp.where(lev == 0, 0, 24)
    above = jnp.where(level == top, 0.0, 0.1).astype(F32)
    below = jnp.where(level == bottom, 0.0, 0.1).astype(F32)

    first_row = jnp.where(gy == 0, 5, 0)
    last_row = jnp.where(gy == NGY - 1, 10, 15)

    def inside(e):
        keep = jnp.logical_and(e >= first_row, e <= last_row)
        return jnp.where(keep, 1.0, 0.0).astype(F32)

    for copy in copies:
        copy.wait()
    for copy in own:
        copy.start()
    for copy in own:
        copy.wait()

    for f in range(FIELDS):
        d = DEPTH[f]
        for e in range(5 - d, 11 + d):
            if 5 <= e < 11:
                u, (at, width) = e - 5, SEG_ROW[f]
            elif e < 5:
                u, (at, width) = 6, SEG_CORNER[f, 5 - e]
            else:
                u, (at, width) = 7, SEG_CORNER[f, e - 10]
            if f < 5:
                body = cw[f, e]
            else:
                body = jnp.concatenate([im[f - 5, e], jnp.zeros((24, 32), F32)], axis=1)
            left = pltpu.roll(xv[0, u], (128 - width - at) % 128, 1)
            right = pltpu.roll(xv[1, u], (COLS - at) % 128, 1)
            halo = jnp.where(lane >= 112, left, right)
            value = jnp.where(lane < COLS, body, halo)
            if not 5 <= e < 11 and f not in (3, 4):
                value = value * inside(e)
            q[f, e] = value

    def east(x):
        return pltpu.roll(x, 127, 1)

    def west(x):
        return pltpu.roll(x, 1, 1)

    def vertical(x):
        return pltpu.roll(x, 23, 0) * above + pltpu.roll(x, 1, 0) * below

    def forward(ref, base, v, e, wu, wv):
        k = MIX[v]
        x = ref[base + v, e]
        total = (1.0 - 4.0 * k - 0.2) * x + vertical(x)
        total += (k - wu) * east(x) + (k + wu) * west(x)
        total += (k - wv) * ref[base + v, e + 1] + (k + wv) * ref[base + v, e - 1]
        return x, total

    def adjoint(ref, v, e, wu, wn, ws):
        k = MIX[v]
        x = ref[v, e]
        total = (1.0 - 4.0 * k - 0.2) * x + vertical(x)
        total += east((k + wu) * x) + west((k - wu) * x)
        total += (k + wn) * ref[v, e + 1] + (k - ws) * ref[v, e - 1]
        return x, total

    def slope(x):
        t = jnp.tanh(x)
        return t, 0.3 - 0.3 * t * t

    def winds(e):
        return 0.125 * q[3, e], 0.125 * q[4, e]

    def stage_one(e, carry):
        wu, wv = winds(e)
        keep = inside(e)
        for v in range(VARS):
            _, s = slope(q[v, e])
            sc[v, e] = s
            x, total = forward(q, 5, v, e, wu, wv)
            d1[v, e] = (total - s * x) * keep
        return carry

    lax.fori_loop(1, 15, stage_one, 0)

    def stage_path(e, carry):
        wu, wv = winds(e)
        for v in range(VARS):
            x, total = forward(q, 0, v, e, wu, wv)
            _, s = slope(total - 0.3 * jnp.tanh(x))
            st[v, e] = s
        return carry

    lax.fori_loop(2, 14, stage_path, 0)

    def stage_two(e, carry):
        wu, wv = winds(e)
        keep = inside(e)
        for v in range(VARS):
            x, total = forward(d1, 0, v, e, wu, wv)
            res[v, e] = (total - st[v, e] * x - q[8 + v, e]) * keep
        return carry

    lax.fori_loop(2, 14, stage_two, 0)

    def stage_three(e, carry):
        wu, _ = winds(e)
        keep = inside(e)
        wn, ws = 0.125 * q[4, e + 1], 0.125 * q[4, e - 1]
        for v in range(VARS):
            x, total = adjoint(res, v, e, wu, wn, ws)
            a1[v, e] = (total - st[v, e] * x) * keep
        return carry

    lax.fori_loop(3, 13, stage_three, 0)

    def stage_four(e, carry):
        wu, _ = winds(e)
        keep = inside(e)
        wn, ws = 0.125 * q[4, e + 1], 0.125 * q[4, e - 1]
        for v in range(VARS):
            x, total = adjoint(a1, v, e, wu, wn, ws)
            start = q[5 + v, e]
            slant = start + total - sc[v, e] * x
            up[v, e - 4] = (start - 0.5 * slant) * keep
            q[v, e] = slant
        return carry

    lax.fori_loop(4, 12, stage_four, 0)
    for v in range(VARS):
        for j in range(ROWS):
            grad[v, j] = q[v, 5 + j, 0:16, 0:COLS]
    grad_copy = pltpu.make_async_copy(grad, gradient, out_sem.at[3])
    grad_copy.start()

    pieces = ((0.375, 0.625, 0.0), (0.125, 0.875, 0.0), (0.0, 0.875, 0.125), (0.0, 0.625, 0.375))
    low, high = inside(4), inside(11)
    for v in range(VARS):
        rows = [up[v, e] for e in range(8)]
        for r in range(-1, 25):
            j, a = r // 4, r % 4
            c = pieces[a]
            value = c[1] * rows[j + 1]
            if c[0]:
                value += c[0] * rows[j]
            else:
                value += c[2] * rows[j + 2]
            if r == -1:
                value = value * low
            if r == 24:
                value = value * high
            vr[v, pl.ds((r % 32) * 24, 24), :] = value

    for copy in late:
        copy.wait()

    sub = lax.broadcasted_iota(jnp.int32, (8, FCOLS), 0)
    lane_edge = lax.broadcasted_iota(jnp.int32, (24, 128), 1)
    for v in range(VARS):
        for l in range(LEVS):
            lhs[pl.ds(32 * l, 32), :] = vr[v, pl.ds(l, 32, stride=24), :]
        lhs[pl.ds(512, 32), :] = vr[v, pl.ds(16 + 7 * lev, 32, stride=24), :]
        fi[...] = split_dot(lhs[...], table[...])

        def add_state(l, carry):
            base = pl.multiple_of(32 * l, 32)
            fn[v, l + 1, 0:24, 0:FCOLS] += fi[pl.ds(base, 24), 0:FCOLS]
            south = jnp.broadcast_to(fyv[0, v, pl.ds(l, 1), :] * low, (8, FCOLS))
            north = jnp.broadcast_to(fyv[1, v, pl.ds(l, 1), :] * high, (8, FCOLS))
            edge = jnp.where(sub == 0, north, jnp.where(sub == 7, south, 0.0))
            fn[v, l + 1, 24:32, 0:FCOLS] = edge + fi[pl.ds(base + 24, 8), 0:FCOLS]
            for t in range(3):
                n = 3 * l + t
                left = pltpu.roll(fxv[0, v], 127 - n, 1)
                right = pltpu.roll(fxv[1, v], lax.rem(128 - n, 128), 1)
                side = jnp.where(lane8 == 0, right, jnp.where(lane8 == 127, left, 0.0))
                fn[v, l + 1, 8 * t : 8 * t + 8, FCOLS:512] = (
                    side + fi[pl.ds(base + 8 * t, 8), FCOLS:512]
                )
            return carry

        lane8 = lane_edge[0:8]
        lax.fori_loop(0, LEVS, add_state, 0)
        fn[v, other, 0:24, 0:FCOLS] += fi[512:536, 0:FCOLS]

    outs = []
    for v in range(VARS):
        k = MIX[v]

        def step(l, carry):
            x = fn[v, l + 1, 0:24, 0:FCOLS]
            whole = fn[v, l + 1, 0:24, :]
            tall = fn[v, l + 1, :, 0:FCOLS]
            wu, wv = 0.125 * wf[0, l], 0.125 * wf[1, l]
            total = (1.0 - 4.0 * k - 0.2) * x - 0.3 * jnp.tanh(x)
            total += 0.1 * (fn[v, l, 0:24, 0:FCOLS] + fn[v, l + 2, 0:24, 0:FCOLS])
            total += (k - wu) * pltpu.roll(whole, 511, 1)[:, 0:FCOLS]
            total += (k + wu) * pltpu.roll(whole, 1, 1)[:, 0:FCOLS]
            total += (k - wv) * pltpu.roll(tall, 31, 0)[0:24]
            total += (k + wv) * pltpu.roll(tall, 1, 0)[0:24]
            out[v, l] = total
            return carry

        lax.fori_loop(0, LEVS, step, 0)
        copy = pltpu.make_async_copy(out.at[v], fine_next.at[v], out_sem.at[v])
        copy.start()
        outs.append(copy)
    for copy in outs:
        copy.wait()
    grad_copy.wait()


def solve(*args):
    line = lambda n: pltpu.VMEM((n, 16, 24, 128), F32)
    return pl.pallas_call(
        solve_kernel,
        out_shape=(
            jax.ShapeDtypeStruct((VARS, LEVS, FROWS, FCOLS), F32),
            jax.ShapeDtypeStruct((VARS, ROWS, LEVS, COLS), F32),
        ),
        in_specs=[ANY] * 10,
        out_specs=(ANY, ANY),
        scratch_shapes=[
            line(5),
            pltpu.VMEM((6, 16, 24, COLS), F32),
            pltpu.VMEM((2, 8, 24, 128), F32),
            pltpu.VMEM((2, VARS, LEVS, FCOLS), F32),
            pltpu.VMEM((2, VARS, 8, 128), F32),
            pltpu.VMEM((VARS, 18, 32, 512), F32),
            pltpu.VMEM((2, LEVS, FROWS, FCOLS), F32),
            line(FIELDS), line(3), line(3), line(3), line(3), line(3),
            pltpu.VMEM((VARS, 8, 24, 128), F32),
            pltpu.VMEM((VARS, 32 * 24, 128), F32),
            pltpu.VMEM((17 * 32, 128), F32),
            pltpu.VMEM((17 * 32, 512), F32),
            pltpu.VMEM((128, 512), BF16),
            pltpu.VMEM((VARS, ROWS, LEVS, COLS), F32),
            pltpu.VMEM((VARS, LEVS, FROWS, FCOLS), F32),
            pltpu.SemaphoreType.DMA((12,)),
            pltpu.SemaphoreType.DMA((4,)),
        ],
        name="solve",
    )(*args)


def per_device(fine_state, wind_field, increment, misfit):
    inc = jnp.transpose(increment, (0, 2, 1, 3))
    mis = jnp.transpose(misfit, (0, 2, 1, 3))
    halos = exchange(fine_state, wind_field, inc, mis)
    fine_next, gradient = solve(fine_state, wind_field, inc, mis, *halos)
    return fine_next, jnp.transpose(gradient, (0, 2, 1, 3))


def solution(mesh):
    spec = P(None, "lev", "gy", "gx")
    return jax.shard_map(
        per_device, mesh=mesh, in_specs=(spec,) * 4, out_specs=(spec, spec), check_vma=False
    )
```

```python
import functools

import jax
import jax.numpy as jnp
from jax import lax
from jax.experimental import pallas as pl
from jax.experimental.pallas import tpu as pltpu
from jax.sharding import PartitionSpec as P

MESH = pl.DeviceIdType.MESH
F32 = jnp.float32
BF16 = jnp.bfloat16
HBM = pl.BlockSpec(memory_space=pltpu.HBM)
VMEM = pl.BlockSpec(memory_space=pltpu.VMEM)

MIX = (0.05, 0.1, 0.2)
VARS, LEVS, ROWS, COLS = 3, 16, 6, 96
FROWS, FCOLS = 24, 384
NGX, NGY = 4, 16

DEPTH = (4, 4, 4, 4, 4, 5, 5, 5, 3, 3, 3)
FIELDS = len(DEPTH)


def segments_row():
    place, at = {}, 0
    for f in range(FIELDS):
        place[f] = (at, DEPTH[f])
        at += DEPTH[f]
    return place


def segments_corner():
    place, at = {}, 0
    for f in range(FIELDS):
        for k in range(1, DEPTH[f] + 1):
            place[f, k] = (at, DEPTH[f] + 1 - k)
            at += DEPTH[f] + 1 - k
    return place


SEG_ROW = segments_row()
SEG_CORNER = segments_corner()


ITEMS = [(f, k) for f in range(5, FIELDS) for k in range(1, DEPTH[f] + 1)]
EARLY = 3 * len(ITEMS) // 4
ITEMS += [(f, k) for f in range(5) for k in range(1, DEPTH[f] + 1)]
UNITS = 3 * len(ITEMS) // 4


def two_parts(x):
    high = x.astype(BF16)
    return high, (x - high.astype(F32)).astype(BF16)


def exchange_kernel(
    fine, wind, inc, mis,
    fs, wf, base, yp, cwo, imo, xm, table_a, table_b,
    half, ys, xs, fys, fy, fxs, fx, fl, table,
    load_sem, ready, send_sem, recv_sem,
):
    gx, gy, lev = lax.axis_index("gx"), lax.axis_index("gy"), lax.axis_index("lev")
    gxs = (lax.rem(gx + 1, NGX), lax.rem(gx + NGX - 1, NGX))
    gys = (lax.rem(gy + 1, NGY), lax.rem(gy + NGY - 1, NGY))
    partner = (gx, gy, 1 - lev)
    near = [(gx, gys[0], lev), (gx, gys[1], lev), (gxs[0], gy, lev), (gxs[1], gy, lev)]

    barrier = pltpu.get_barrier_semaphore()
    for device in near + [partner]:
        pl.semaphore_signal(barrier, inc=1, device_id=device, device_id_type=MESH)

    loads = [
        pltpu.make_async_copy(inc, imo.at[0:3, :, 0:16, :], load_sem.at[5]),
        pltpu.make_async_copy(mis, imo.at[3:6, :, 0:16, :], load_sem.at[6]),
    ]
    for f in range(VARS):
        loads.append(pltpu.make_async_copy(fine.at[f], fs.at[f], load_sem.at[f]))
    for f in range(2):
        loads.append(pltpu.make_async_copy(wind.at[f], wf.at[f], load_sem.at[3 + f]))
    for copy in loads:
        copy.start()

    source = lax.broadcasted_iota(jnp.int32, (FCOLS, 128), 0) // 4
    target = lax.broadcasted_iota(jnp.int32, (FCOLS, 128), 1)
    table[...] = jnp.where(source == target, 0.0625, 0.0).astype(BF16)

    started = []

    def send(src, dst, device):
        i = len(started)
        copy = pltpu.make_async_remote_copy(
            src_ref=src, dst_ref=dst, send_sem=send_sem.at[i], recv_sem=recv_sem.at[i],
            device_id=device, device_id_type=MESH,
        )
        copy.start()
        started.append(copy)
        return copy

    tile = pl.ds(pl.multiple_of((1 - lev) * 8, 8), 8)
    lane = lax.broadcasted_iota(jnp.int32, (LEVS, 128), 1)

    def unit(f, j):
        if f < 5:
            return cwo[f, j, 0:16, :]
        body = imo[f - 5, j, 0:16, :]
        return jnp.concatenate([body, jnp.zeros((LEVS, 128 - COLS), F32)], axis=1)

    def row_of(s, k):
        return ROWS - k if s == 0 else k - 1

    def pack_rows(s, start, stop):
        for g in range(start // 3, stop // 3):
            parts = [unit(f, row_of(s, k)) for f, k in ITEMS[4 * g : 4 * g + 4]]
            for m in range(3):
                rest = pltpu.roll(parts[3], 96 - 32 * m, 1)
                ys[s, 3 * g + m] = jnp.where(lane < COLS, parts[m], rest)

    loads[0].wait()
    loads[1].wait()
    for s in range(2):
        pack_rows(s, 0, EARLY)
    pl.semaphore_wait(barrier, len(near) + 1)
    for s in range(2):
        pl.semaphore_signal(ready, inc=1, device_id=near[s], device_id_type=MESH)
    y_im = [
        send(ys.at[s, 0:EARLY], yp.at[s, 0:EARLY, 0:16, :], near[s]) for s in range(2)
    ]
    own = [send(imo.at[:, :, tile, :], imo.at[:, :, 16:24, :], partner)]

    for v in range(VARS):
        loads[2 + v].wait()
        for l in range(LEVS):
            fys[0, v, l : l + 1, :] = fs[v, l, FROWS - 1 : FROWS, :]
            fys[1, v, l : l + 1, :] = fs[v, l, 0:1, :]
    y_fine = [send(fys.at[s], fy.at[s], near[s]) for s in range(2)]

    def coarsen(f, ref):
        high, low = two_parts(ref.reshape(LEVS * FROWS, FCOLS))
        half[...] = jnp.dot(high, table[...], preferred_element_type=F32) + jnp.dot(
            low, table[...], preferred_element_type=F32
        )
        for j in range(ROWS):
            total = half[pl.ds(4 * j, LEVS, stride=FROWS), :]
            for a in range(1, 4):
                total += half[pl.ds(4 * j + a, LEVS, stride=FROWS), :]
            cwo[f, j, 0:16, :] = total

    for f in range(VARS):
        coarsen(f, fs[f])
    for f in range(2):
        loads[5 + f].wait()
        coarsen(3 + f, wf[f])
    for s in range(2):
        pack_rows(s, EARLY, UNITS)
    y_cw = [
        send(ys.at[s, EARLY:UNITS], yp.at[s, EARLY:UNITS, 0:16, :], near[s])
        for s in range(2)
    ]
    own.append(send(cwo.at[:, :, tile, :], cwo.at[:, :, 16:24, :], partner))

    def packed(out, value, h, at, width):
        first = COLS - width if h == 0 else 0
        moved = pltpu.roll(value, (at - first) % 128, 1)
        return jnp.where(jnp.logical_and(lane >= at, lane < at + width), moved, out)

    zero = jnp.zeros((LEVS, 128), F32)
    for h in range(2):
        for s in range(2):
            out = zero
            for (f, k), (at, width) in SEG_CORNER.items():
                out = packed(out, unit(f, row_of(s, k)), h, at, width)
            xs[h, 6 + s] = out
    pl.semaphore_wait(ready, 2)
    corner = [
        [
            send(xs.at[h, 6 + s], xm.at[h, 6 + s, 0:16, :], (gxs[h], gys[s], lev))
            for s in range(2)
        ]
        for h in range(2)
    ]
    for h in range(2):
        for j in range(ROWS):
            out = zero
            for f, (at, width) in SEG_ROW.items():
                out = packed(out, unit(f, j), h, at, width)
            xs[h, j] = out
    x_row = [send(xs.at[h, 0:6], xm.at[h, 0:6, 0:16, :], near[2 + h]) for h in range(2)]
    edge = 15 * (1 - lev)
    fine_lev = send(fs.at[:, edge], fl, partner)

    lane8 = lax.broadcasted_iota(jnp.int32, (8, 128), 1)
    for v in range(VARS):
        outs = [jnp.zeros((8, 128), F32)] * 2
        for l in range(LEVS):
            for t in range(3):
                n = 3 * l + t
                first = pltpu.roll(fs[v, l, 8 * t : 8 * t + 8, 0:128], n, 1)
                last = pltpu.roll(fs[v, l, 8 * t : 8 * t + 8, 256:384], (n + 1) % 128, 1)
                outs[0] = jnp.where(lane8 == n, last, outs[0])
                outs[1] = jnp.where(lane8 == n, first, outs[1])
        fxs[0, v] = outs[0]
        fxs[1, v] = outs[1]
    x_fine = [send(fxs.at[h], fx.at[h], near[2 + h]) for h in range(2)]

    coarse_lane = lax.broadcasted_iota(jnp.int32, (128, FCOLS), 0)
    fine_col = lax.broadcasted_iota(jnp.int32, (128, FCOLS), 1)

    def columns(shift):
        scaled = 4 * (fine_col + shift) + 10
        beneath = lax.shift_right_arithmetic(scaled, 4)
        fraction = jnp.bitwise_and(scaled, 15).astype(F32) * 0.0625
        first = coarse_lane == jnp.bitwise_and(beneath - 1, 127)
        second = coarse_lane == jnp.bitwise_and(beneath, 127)
        return jnp.where(first, 1.0 - fraction, 0.0) + jnp.where(second, fraction, 0.0)

    middle = columns(0).astype(BF16)
    ahead, behind = columns(1), columns(-1)
    slant = (0.125 * (behind - ahead)).astype(BF16)
    around = (ahead + behind).astype(BF16)
    for part in range(2):
        rows = slice(128 * part, 128 * part + 128)
        table_a[rows, 0:FCOLS] = middle
        table_a[rows, FCOLS:] = slant
        table_b[rows, :] = middle
        table_b[slice(256 + 128 * part, 384 + 128 * part), :] = around

    row = lax.broadcasted_iota(jnp.int32, (FROWS, FCOLS), 0)
    col = lax.broadcasted_iota(jnp.int32, (FROWS, FCOLS), 1)

    def fine_step(l, carry):
        wu, wv = 0.125 * wf[0, l], 0.125 * wf[1, l]
        has_low = jnp.where(l > 0, 0.1, 0.0).astype(F32)
        has_high = jnp.where(l < LEVS - 1, 0.1, 0.0).astype(F32)
        for v in range(VARS):
            k = MIX[v]
            x = fs[v, l]
            total = (1.0 - 4.0 * k - 0.2) * x
            total += has_low * fs[v, jnp.maximum(l - 1, 0)]
            total += has_high * fs[v, jnp.minimum(l + 1, LEVS - 1)]
            total += (k - wu) * jnp.where(col == FCOLS - 1, 0.0, pltpu.roll(x, FCOLS - 1, 1))
            total += (k + wu) * jnp.where(col == 0, 0.0, pltpu.roll(x, 1, 1))
            total += (k - wv) * jnp.where(row == FROWS - 1, 0.0, pltpu.roll(x, FROWS - 1, 0))
            total += (k + wv) * jnp.where(row == 0, 0.0, pltpu.roll(x, 1, 0))
            base[v, l] = total
        return carry

    lax.fori_loop(0, LEVS, fine_step, 0)

    relays = []
    for s in range(2):
        y_im[s].wait_recv()
        relays.append(
            send(yp.at[s, 0:EARLY, tile, :], yp.at[s, 0:EARLY, 16:24, :], partner)
        )
    for copy in y_fine + x_fine + [fine_lev]:
        copy.wait_recv()

    sub8 = lax.broadcasted_iota(jnp.int32, (8, FCOLS), 0)
    not_first = jnp.where(gy == 0, 0.0, 1.0).astype(F32)
    not_last = jnp.where(gy == NGY - 1, 0.0, 1.0).astype(F32)

    def fine_edges(l, carry):
        for v in range(VARS):
            k = MIX[v]
            south = jnp.broadcast_to(fy[0, v, pl.ds(l, 1), :] * not_first, (8, FCOLS))
            north = jnp.broadcast_to(fy[1, v, pl.ds(l, 1), :] * not_last, (8, FCOLS))
            wv0, wv1 = 0.125 * wf[1, l, 0:8], 0.125 * wf[1, l, 16:24]
            base[v, l, 0:8] += jnp.where(sub8 == 0, (k + wv0) * south, 0.0)
            base[v, l, 16:24] += jnp.where(sub8 == 7, (k - wv1) * north, 0.0)
            for t in range(3):
                n = 3 * l + t
                rows = slice(8 * t, 8 * t + 8)
                left = pltpu.roll(fx[0, v], lax.rem(128 - n, 128), 1)
                right = pltpu.roll(fx[1, v], 127 - n, 1)
                wu0, wu1 = 0.125 * wf[0, l, rows, 0:128], 0.125 * wf[0, l, rows, 256:384]
                base[v, l, rows, 0:128] += jnp.where(lane8 == 0, (k + wu0) * left, 0.0)
                base[v, l, rows, 256:384] += jnp.where(lane8 == 127, (k - wu1) * right, 0.0)
        return carry

    lax.fori_loop(0, LEVS, fine_edges, 0)
    for v in range(VARS):
        base[v, edge] += 0.1 * fl[v]

    for s in range(2):
        y_cw[s].wait_recv()
        relays.append(
            send(yp.at[s, EARLY:UNITS, tile, :], yp.at[s, EARLY:UNITS, 16:24, :], partner)
        )
    for h in range(2):
        for s in range(2):
            corner[h][s].wait_recv()
        x_row[h].wait_recv()
        relays.append(send(xm.at[h, :, tile, :], xm.at[h, :, 16:24, :], partner))
    for copy in own + relays:
        copy.wait_recv()
    for copy in started:
        copy.wait_send()


COPIES = 23


def exchange(fine, wind, inc, mis):
    return pl.pallas_call(
        exchange_kernel,
        out_shape=(
            pltpu.VMEM((VARS, LEVS, FROWS, FCOLS), F32),
            pltpu.VMEM((2, LEVS, FROWS, FCOLS), F32),
            pltpu.VMEM((VARS, LEVS, FROWS, FCOLS), F32),
            pltpu.VMEM((2, UNITS, 24, 128), F32),
            pltpu.VMEM((5, ROWS, 24, 128), F32),
            pltpu.VMEM((6, ROWS, 24, COLS), F32),
            pltpu.VMEM((2, 8, 24, 128), F32),
            pltpu.VMEM((256, 2 * FCOLS), BF16),
            pltpu.VMEM((512, FCOLS), BF16),
        ),
        in_specs=[HBM] * 4,
        out_specs=(VMEM,) * 9,
        scratch_shapes=[
            pltpu.VMEM((LEVS * FROWS, 128), F32),
            pltpu.VMEM((2, UNITS, LEVS, 128), F32),
            pltpu.VMEM((2, 8, LEVS, 128), F32),
            pltpu.VMEM((2, VARS, LEVS, FCOLS), F32),
            pltpu.VMEM((2, VARS, LEVS, FCOLS), F32),
            pltpu.VMEM((2, VARS, 8, 128), F32),
            pltpu.VMEM((2, VARS, 8, 128), F32),
            pltpu.VMEM((VARS, FROWS, FCOLS), F32),
            pltpu.VMEM((FCOLS, 128), BF16),
            pltpu.SemaphoreType.DMA((7,)),
            pltpu.SemaphoreType.REGULAR,
            pltpu.SemaphoreType.DMA((COPIES,)),
            pltpu.SemaphoreType.DMA((COPIES,)),
        ],
        compiler_params=pltpu.CompilerParams(
            vmem_limit_bytes=20 << 20, collective_id=0, has_side_effects=True
        ),
        name="exchange",
    )(fine, wind, inc, mis)


def solve_kernel(
    fs, wf, base, yp, cwo, imo, xm, table_a, table_b,
    fine_next, gradient,
    q, st, sc, d1, res, a1, up, vr, lv, ly, grad, out, out_sem,
):
    gy, lev = lax.axis_index("gy"), lax.axis_index("lev")
    lane = lax.broadcasted_iota(jnp.int32, (24, 128), 1)
    level = lax.broadcasted_iota(jnp.int32, (24, 128), 0)
    top = jnp.where(lev == 1, 15, 24)
    bottom = jnp.where(lev == 0, 0, 24)
    above = jnp.where(level == top, 0.0, 0.1).astype(F32)
    below = jnp.where(level == bottom, 0.0, 0.1).astype(F32)

    first_row = jnp.where(gy == 0, 5, 0)
    last_row = jnp.where(gy == NGY - 1, 10, 15)

    def inside(e):
        keep = jnp.logical_and(e >= first_row, e <= last_row)
        return jnp.where(keep, 1.0, 0.0).astype(F32)

    def fill(f, e, body, u, at, width):
        left = pltpu.roll(xm[0, u], (128 - width - at) % 128, 1)
        right = pltpu.roll(xm[1, u], (COLS - at) % 128, 1)
        value = jnp.where(lane < COLS, body, jnp.where(lane >= 112, left, right))
        if not 5 <= e < 11 and f not in (3, 4):
            value = value * inside(e)
        q[f, e] = value

    for f in range(FIELDS):
        for j in range(ROWS):
            if f < 5:
                body = cwo[f, j]
            else:
                body = jnp.concatenate([imo[f - 5, j], jnp.zeros((24, 32), F32)], axis=1)
            fill(f, 5 + j, body, j, *SEG_ROW[f])
    for s in range(2):
        for i, (f, k) in enumerate(ITEMS):
            g, m = i // 4, i % 4
            if m < 3:
                body = yp[s, 3 * g + m]
            else:
                pieces = [pltpu.roll(yp[s, 3 * g + n], 32 + 32 * n, 1) for n in range(3)]
                body = jnp.where(
                    lane < 32, pieces[0], jnp.where(lane < 64, pieces[1], pieces[2])
                )
            fill(f, 5 - k if s == 0 else 10 + k, body, 6 + s, *SEG_CORNER[f, k])

    def east(x):
        return pltpu.roll(x, 127, 1)

    def west(x):
        return pltpu.roll(x, 1, 1)

    def vertical(x):
        return pltpu.roll(x, 23, 0) * above + pltpu.roll(x, 1, 0) * below

    def forward(ref, base, v, e, wu, wv):
        k = MIX[v]
        x = ref[base + v, e]
        total = (1.0 - 4.0 * k - 0.2) * x + vertical(x)
        total += (k - wu) * east(x) + (k + wu) * west(x)
        total += (k - wv) * ref[base + v, e + 1] + (k + wv) * ref[base + v, e - 1]
        return x, total

    def adjoint(ref, v, e, wu, wn, ws):
        k = MIX[v]
        x = ref[v, e]
        total = (1.0 - 4.0 * k - 0.2) * x + vertical(x)
        total += east((k + wu) * x) + west((k - wu) * x)
        total += (k + wn) * ref[v, e + 1] + (k - ws) * ref[v, e - 1]
        return x, total

    def slope(x):
        t = jnp.tanh(x)
        return t, 0.3 - 0.3 * t * t

    def winds(e):
        return 0.125 * q[3, e], 0.125 * q[4, e]

    def stage_one(e, carry):
        wu, wv = winds(e)
        keep = inside(e)
        for v in range(VARS):
            _, s = slope(q[v, e])
            sc[v, e] = s
            x, total = forward(q, 5, v, e, wu, wv)
            d1[v, e] = (total - s * x) * keep
        return carry

    for e in range(1, 15):
        stage_one(e, 0)

    def stage_path(e, carry):
        wu, wv = winds(e)
        for v in range(VARS):
            x, total = forward(q, 0, v, e, wu, wv)
            _, s = slope(total - 0.3 * jnp.tanh(x))
            st[v, e] = s
        return carry

    for e in range(2, 14):
        stage_path(e, 0)

    def stage_two(e, carry):
        wu, wv = winds(e)
        keep = inside(e)
        for v in range(VARS):
            x, total = forward(d1, 0, v, e, wu, wv)
            res[v, e] = (total - st[v, e] * x - q[8 + v, e]) * keep
        return carry

    for e in range(2, 14):
        stage_two(e, 0)

    def stage_three(e, carry):
        wu, _ = winds(e)
        keep = inside(e)
        wn, ws = 0.125 * q[4, e + 1], 0.125 * q[4, e - 1]
        for v in range(VARS):
            x, total = adjoint(res, v, e, wu, wn, ws)
            a1[v, e] = (total - st[v, e] * x) * keep
        return carry

    for e in range(3, 13):
        stage_three(e, 0)

    def stage_four(e, carry):
        wu, _ = winds(e)
        keep = inside(e)
        wn, ws = 0.125 * q[4, e + 1], 0.125 * q[4, e - 1]
        for v in range(VARS):
            x, total = adjoint(a1, v, e, wu, wn, ws)
            start = q[5 + v, e]
            slant = start + total - sc[v, e] * x
            up[v, e - 4] = (start - 0.5 * slant) * keep
            q[v, e] = slant
        return carry

    for e in range(4, 12):
        stage_four(e, 0)
    for v in range(VARS):
        for j in range(ROWS):
            grad[v, j] = q[v, 5 + j, 0:16, 0:COLS]
    grad_copy = pltpu.make_async_copy(grad, gradient, out_sem.at[6])
    grad_copy.start()

    pieces = ((0.375, 0.625, 0.0), (0.125, 0.875, 0.0), (0.0, 0.875, 0.125), (0.0, 0.625, 0.375))
    low, high = inside(4), inside(11)
    outs = []
    for v in range(VARS):
        k = MIX[v]
        rows = [up[v, e] for e in range(8)]

        def fine_row(r):
            j, a = r // 4, r % 4
            c = pieces[a]
            value = c[1] * rows[j + 1]
            value += c[0] * rows[j] if c[0] else c[2] * rows[j + 2]
            if r == -1:
                value = value * low
            if r == 24:
                value = value * high
            return value

        south, here = fine_row(-1), fine_row(0)
        for r in range(FROWS):
            north = fine_row(r + 1)
            mixed = ((0.8 - 4.0 * k) / k) * here + (north + south) + (1.0 / k) * vertical(here)
            at = pl.ds(24 * r, LEVS)
            vr[0, at, :] = here[0:16]
            vr[1, at, :] = mixed[0:16]
            vr[2, at, :] = 0.125 * (south - north)[0:16]
            south, here = here, north
        for l in range(LEVS):
            at = pl.ds(24 * l, 24)
            by_level = pl.ds(l, 24, stride=24)
            lv[at, 256:384], lv[at, 384:512] = two_parts(vr[0, by_level, :])
            lv[at, 0:128], lv[at, 128:256] = two_parts(vr[1, by_level, :])
            ly[at, 0:128], ly[at, 128:256] = two_parts(vr[2, by_level, :])
        for c in range(2):
            at = slice(192 * c, 192 * c + 192)
            levels = slice(8 * c, 8 * c + 8)
            shape = (8, FROWS, FCOLS)

            def dot(x, t):
                return jnp.dot(x, t, preferred_element_type=F32).reshape(shape)

            step = dot(lv[at, 256:512], table_a[:, 0:FCOLS])
            total = base[v, levels] - 0.3 * jnp.tanh(fs[v, levels] + step)
            total += k * dot(lv[at, :], table_b[...])
            total += wf[0, levels] * dot(lv[at, 256:512], table_a[:, FCOLS:])
            total += wf[1, levels] * dot(ly[at, :], table_a[:, 0:FCOLS])
            out[v, levels] = total
            copy = pltpu.make_async_copy(
                out.at[v, levels], fine_next.at[v, levels], out_sem.at[2 * v + c]
            )
            copy.start()
            outs.append(copy)
    for copy in outs:
        copy.wait()
    grad_copy.wait()


def solve(*args):
    line = lambda n: pltpu.VMEM((n, 16, 24, 128), F32)
    return pl.pallas_call(
        solve_kernel,
        out_shape=(
            jax.ShapeDtypeStruct((VARS, LEVS, FROWS, FCOLS), F32),
            jax.ShapeDtypeStruct((VARS, ROWS, LEVS, COLS), F32),
        ),
        in_specs=[VMEM] * 9,
        out_specs=(HBM, HBM),
        scratch_shapes=[
            line(FIELDS), line(3), line(3), line(3), line(3), line(3),
            pltpu.VMEM((VARS, 8, 24, 128), F32),
            pltpu.VMEM((3, 24 * 24, 128), F32),
            pltpu.VMEM((LEVS * FROWS, 512), BF16),
            pltpu.VMEM((LEVS * FROWS, 256), BF16),
            pltpu.VMEM((VARS, ROWS, LEVS, COLS), F32),
            pltpu.VMEM((VARS, LEVS, FROWS, FCOLS), F32),
            pltpu.SemaphoreType.DMA((7,)),
        ],
        compiler_params=pltpu.CompilerParams(vmem_limit_bytes=40 << 20),
        name="solve",
    )(*args)


def per_device(fine_state, wind_field, increment, misfit):
    inc = jnp.transpose(increment, (0, 2, 1, 3))
    mis = jnp.transpose(misfit, (0, 2, 1, 3))
    held = [pltpu.with_memory_space_constraint(x, pltpu.HBM) for x in (fine_state, wind_field, inc, mis)]
    fine_next, gradient = solve(*exchange(*held))
    return fine_next, jnp.transpose(gradient, (0, 2, 1, 3))


def solution(mesh):
    spec = P(None, "lev", "gy", "gx")
    return jax.shard_map(
        per_device, mesh=mesh, in_specs=(spec,) * 4, out_specs=(spec, spec), check_vma=False
    )
```

```python
import functools

import jax
import jax.numpy as jnp
from jax import lax
from jax.experimental import pallas as pl
from jax.experimental.pallas import tpu as pltpu
from jax.sharding import PartitionSpec as P

MESH = pl.DeviceIdType.MESH
F32 = jnp.float32
BF16 = jnp.bfloat16
HBM = pl.BlockSpec(memory_space=pltpu.HBM)
VMEM = pl.BlockSpec(memory_space=pltpu.VMEM)

MIX = (0.05, 0.1, 0.2)
VARS, LEVS, ROWS, COLS = 3, 16, 6, 96
FROWS, FCOLS = 24, 384
NGX, NGY = 4, 16

DEPTH = (4, 4, 4, 4, 4, 5, 5, 5, 3, 3, 3)
FIELDS = len(DEPTH)


def segments_row():
    place, at = {}, 0
    for f in range(FIELDS):
        place[f] = (at, DEPTH[f])
        at += DEPTH[f]
    return place


def segments_corner():
    place, at = {}, 0
    for f in range(FIELDS):
        for k in range(1, DEPTH[f] + 1):
            place[f, k] = (at, DEPTH[f] + 1 - k)
            at += DEPTH[f] + 1 - k
    return place


SEG_ROW = segments_row()
SEG_CORNER = segments_corner()


ITEMS = [(f, k) for f in range(5, FIELDS) for k in range(1, DEPTH[f] + 1)]
EARLY = 3 * len(ITEMS) // 4
ITEMS += [(f, k) for f in range(5) for k in range(1, DEPTH[f] + 1)]
UNITS = 3 * len(ITEMS) // 4


def two_parts(x):
    high = x.astype(BF16)
    return high, (x - high.astype(F32)).astype(BF16)


def exchange_kernel(
    fine, wind, inc, mis,
    fs, wf, base, yp, cwo, imo, xm, table_a, table_b,
    half, ys, xs, fys, fy, fxs, fx, fl, table,
    load_sem, answer, ready, send_sem, recv_sem,
):
    gx, gy, lev = lax.axis_index("gx"), lax.axis_index("gy"), lax.axis_index("lev")
    gxs = (lax.rem(gx + 1, NGX), lax.rem(gx + NGX - 1, NGX))
    gys = (lax.rem(gy + 1, NGY), lax.rem(gy + NGY - 1, NGY))
    partner = (gx, gy, 1 - lev)
    near = [(gx, gys[0], lev), (gx, gys[1], lev), (gxs[0], gy, lev), (gxs[1], gy, lev)]

    has_next, has_last = gy < NGY - 1, gy > 0
    going, coming = (has_next, has_last), (has_last, has_next)
    rows_near = has_next.astype(jnp.int32) + has_last.astype(jnp.int32)

    def signal(semaphore, device, condition=None):
        def act():
            pl.semaphore_signal(semaphore, inc=1, device_id=device, device_id_type=MESH)

        act() if condition is None else pl.when(condition)(act)

    barrier = pltpu.get_barrier_semaphore()
    for s in range(2):
        signal(barrier, near[s], going[s])
    signal(barrier, partner)
    signal(barrier, near[2], gx < NGX - 1)
    signal(barrier, near[3], gx == 0)
    greeted = (gx > 0).astype(jnp.int32) + (gx == NGX - 1).astype(jnp.int32)
    answered = (gx < NGX - 1).astype(jnp.int32) + (gx == 0).astype(jnp.int32)

    loads = [
        pltpu.make_async_copy(inc, imo.at[0:3, :, 0:16, :], load_sem.at[5]),
        pltpu.make_async_copy(mis, imo.at[3:6, :, 0:16, :], load_sem.at[6]),
    ]
    for f in range(VARS):
        loads.append(pltpu.make_async_copy(fine.at[f], fs.at[f], load_sem.at[f]))
    for f in range(2):
        loads.append(pltpu.make_async_copy(wind.at[f], wf.at[f], load_sem.at[3 + f]))
    for copy in loads:
        copy.start()

    source = lax.broadcasted_iota(jnp.int32, (FCOLS, 128), 0) // 4
    target = lax.broadcasted_iota(jnp.int32, (FCOLS, 128), 1)
    table[...] = jnp.where(source == target, 0.0625, 0.0).astype(BF16)

    started = []

    def when(condition, act):
        act() if condition is None else pl.when(condition)(act)

    def send(src, dst, device, goes=None, comes=None):
        i = len(started)
        copy = pltpu.make_async_remote_copy(
            src_ref=src, dst_ref=dst, send_sem=send_sem.at[i], recv_sem=recv_sem.at[i],
            device_id=device, device_id_type=MESH,
        )
        when(goes, copy.start)
        started.append((copy, goes))
        return copy, comes

    def arrive(message):
        when(message[1], message[0].wait_recv)

    def send_row(src, dst, s):
        return send(src, dst, near[s], going[s], coming[s])

    def relay(ref, at, comes=None):
        dst = ref.at[(*at, slice(16, 24), slice(None))]
        return send(ref.at[(*at, tile, slice(None))], dst, partner, comes, comes)

    tile = pl.ds(pl.multiple_of((1 - lev) * 8, 8), 8)
    lane = lax.broadcasted_iota(jnp.int32, (LEVS, 128), 1)

    def unit(f, j):
        if f < 5:
            return cwo[f, j, 0:16, :]
        body = imo[f - 5, j, 0:16, :]
        return jnp.concatenate([body, jnp.zeros((LEVS, 128 - COLS), F32)], axis=1)

    def row_of(s, k):
        return ROWS - k if s == 0 else k - 1

    def pack_rows(s, start, stop):
        for g in range(start // 3, stop // 3):
            parts = [unit(f, row_of(s, k)) for f, k in ITEMS[4 * g : 4 * g + 4]]
            for m in range(3):
                rest = pltpu.roll(parts[3], 96 - 32 * m, 1)
                ys[s, 3 * g + m] = jnp.where(lane < COLS, parts[m], rest)

    loads[0].wait()
    loads[1].wait()
    for s in range(2):
        pack_rows(s, 0, EARLY)
    pl.semaphore_wait(barrier, rows_near + greeted + 1)
    y_im = [send_row(ys.at[s, 0:EARLY], yp.at[s, 0:EARLY, 0:16, :], s) for s in range(2)]
    signal(answer, near[3], gx > 0)
    signal(answer, near[2], gx == NGX - 1)
    own = [send(imo.at[:, :, tile, :], imo.at[:, :, 16:24, :], partner)]

    def coarsen(f, ref):
        high, low = two_parts(ref.reshape(LEVS * FROWS, FCOLS))
        half[...] = jnp.dot(high, table[...], preferred_element_type=F32) + jnp.dot(
            low, table[...], preferred_element_type=F32
        )
        for j in range(ROWS):
            total = half[pl.ds(4 * j, LEVS, stride=FROWS), :]
            for a in range(1, 4):
                total += half[pl.ds(4 * j + a, LEVS, stride=FROWS), :]
            cwo[f, j, 0:16, :] = total

    for f in range(VARS):
        loads[2 + f].wait()
        coarsen(f, fs[f])
    for f in range(2):
        loads[5 + f].wait()
        coarsen(3 + f, wf[f])
    for s in range(2):
        pack_rows(s, EARLY, UNITS)
    y_cw = [
        send_row(ys.at[s, EARLY:UNITS], yp.at[s, EARLY:UNITS, 0:16, :], s) for s in range(2)
    ]
    own.append(send(cwo.at[:, :, tile, :], cwo.at[:, :, 16:24, :], partner))

    def packed(out, value, h, at, width):
        first = COLS - width if h == 0 else 0
        moved = pltpu.roll(value, (at - first) % 128, 1)
        return jnp.where(jnp.logical_and(lane >= at, lane < at + width), moved, out)

    zero = jnp.zeros((LEVS, 128), F32)
    for h in range(2):
        for s in range(2):
            out = zero
            for (f, k), (at, width) in SEG_CORNER.items():
                out = packed(out, unit(f, row_of(s, k)), h, at, width)
            xs[h, 6 + s] = out
    for h in range(2):
        for j in range(ROWS):
            out = zero
            for f, (at, width) in SEG_ROW.items():
                out = packed(out, unit(f, j), h, at, width)
            xs[h, j] = out
    pl.when(answered > 0)(lambda: pl.semaphore_wait(answer, answered))
    for s in range(2):
        signal(ready, near[s], going[s])
    x_row = [send(xs.at[h, 0:6], xm.at[h, 0:6, 0:16, :], near[2 + h]) for h in range(2)]
    edge = 15 * (1 - lev)
    fine_lev = send(fs.at[:, edge], fl, partner)

    for v in range(VARS):
        for l in range(LEVS):
            fys[0, v, l : l + 1, :] = fs[v, l, FROWS - 1 : FROWS, :]
            fys[1, v, l : l + 1, :] = fs[v, l, 0:1, :]
    y_fine = [send_row(fys.at[s], fy.at[s], s) for s in range(2)]

    lane8 = lax.broadcasted_iota(jnp.int32, (8, 128), 1)
    for v in range(VARS):
        outs = [jnp.zeros((8, 128), F32)] * 2
        for l in range(LEVS):
            for t in range(3):
                n = 3 * l + t
                first = pltpu.roll(fs[v, l, 8 * t : 8 * t + 8, 0:128], n, 1)
                last = pltpu.roll(fs[v, l, 8 * t : 8 * t + 8, 256:384], (n + 1) % 128, 1)
                outs[0] = jnp.where(lane8 == n, last, outs[0])
                outs[1] = jnp.where(lane8 == n, first, outs[1])
        fxs[0, v] = outs[0]
        fxs[1, v] = outs[1]
    x_fine = [send(fxs.at[h], fx.at[h], near[2 + h]) for h in range(2)]
    pl.semaphore_wait(ready, rows_near)
    corner = [
        [
            send(
                xs.at[h, 6 + s], xm.at[h, 6 + s, 0:16, :], (gxs[h], gys[s], lev),
                going[s], coming[s],
            )
            for s in range(2)
        ]
        for h in range(2)
    ]

    coarse_lane = lax.broadcasted_iota(jnp.int32, (128, FCOLS), 0)
    fine_col = lax.broadcasted_iota(jnp.int32, (128, FCOLS), 1)

    def columns(shift):
        scaled = 4 * (fine_col + shift) + 10
        beneath = lax.shift_right_arithmetic(scaled, 4)
        fraction = jnp.bitwise_and(scaled, 15).astype(F32) * 0.0625
        first = coarse_lane == jnp.bitwise_and(beneath - 1, 127)
        second = coarse_lane == jnp.bitwise_and(beneath, 127)
        return jnp.where(first, 1.0 - fraction, 0.0) + jnp.where(second, fraction, 0.0)

    middle = columns(0).astype(BF16)
    ahead, behind = columns(1), columns(-1)
    slant = (0.125 * (behind - ahead)).astype(BF16)
    around = (ahead + behind).astype(BF16)
    for part in range(2):
        rows = slice(128 * part, 128 * part + 128)
        table_a[rows, 0:FCOLS] = middle
        table_a[rows, FCOLS:] = slant
        table_b[rows, :] = middle
        table_b[slice(256 + 128 * part, 384 + 128 * part), :] = around

    row = lax.broadcasted_iota(jnp.int32, (FROWS, FCOLS), 0)
    col = lax.broadcasted_iota(jnp.int32, (FROWS, FCOLS), 1)

    def fine_step(l, carry):
        wu, wv = 0.125 * wf[0, l], 0.125 * wf[1, l]
        has_low = jnp.where(l > 0, 0.1, 0.0).astype(F32)
        has_high = jnp.where(l < LEVS - 1, 0.1, 0.0).astype(F32)
        for v in range(VARS):
            k = MIX[v]
            x = fs[v, l]
            total = (1.0 - 4.0 * k - 0.2) * x
            total += has_low * fs[v, jnp.maximum(l - 1, 0)]
            total += has_high * fs[v, jnp.minimum(l + 1, LEVS - 1)]
            total += (k - wu) * jnp.where(col == FCOLS - 1, 0.0, pltpu.roll(x, FCOLS - 1, 1))
            total += (k + wu) * jnp.where(col == 0, 0.0, pltpu.roll(x, 1, 1))
            total += (k - wv) * jnp.where(row == FROWS - 1, 0.0, pltpu.roll(x, FROWS - 1, 0))
            total += (k + wv) * jnp.where(row == 0, 0.0, pltpu.roll(x, 1, 0))
            base[v, l] = total
        return carry

    lax.fori_loop(0, LEVS, fine_step, 0)

    relays = []
    for s in range(2):
        arrive(y_im[s])
        relays.append(relay(yp, (s, slice(0, EARLY)), coming[s]))
    for message in x_fine + [fine_lev]:
        arrive(message)

    def fine_columns(l, carry):
        for v in range(VARS):
            k = MIX[v]
            for t in range(3):
                n = 3 * l + t
                rows = slice(8 * t, 8 * t + 8)
                left = pltpu.roll(fx[0, v], lax.rem(128 - n, 128), 1)
                right = pltpu.roll(fx[1, v], 127 - n, 1)
                wu0, wu1 = 0.125 * wf[0, l, rows, 0:128], 0.125 * wf[0, l, rows, 256:384]
                base[v, l, rows, 0:128] += jnp.where(lane8 == 0, (k + wu0) * left, 0.0)
                base[v, l, rows, 256:384] += jnp.where(lane8 == 127, (k - wu1) * right, 0.0)
        return carry

    lax.fori_loop(0, LEVS, fine_columns, 0)
    for v in range(VARS):
        base[v, edge] += 0.1 * fl[v]

    for h in range(2):
        arrive(x_row[h])
        relays.append(relay(xm, (h, slice(0, 6))))
    for s in range(2):
        arrive(y_cw[s])
        relays.append(relay(yp, (s, slice(EARLY, UNITS)), coming[s]))
    for h in range(2):
        for s in range(2):
            arrive(corner[h][s])
            relays.append(relay(xm, (h, 6 + s), coming[s]))

    for message in y_fine:
        arrive(message)
    sub8 = lax.broadcasted_iota(jnp.int32, (8, FCOLS), 0)

    def fine_rows(l, carry):
        for v in range(VARS):
            k = MIX[v]
            south = jnp.broadcast_to(fy[0, v, pl.ds(l, 1), :], (8, FCOLS))
            north = jnp.broadcast_to(fy[1, v, pl.ds(l, 1), :], (8, FCOLS))
            south = jnp.where(jnp.logical_and(sub8 == 0, gy > 0), south, 0.0)
            north = jnp.where(jnp.logical_and(sub8 == 7, gy < NGY - 1), north, 0.0)
            base[v, l, 0:8] += (k + 0.125 * wf[1, l, 0:8]) * south
            base[v, l, 16:24] += (k - 0.125 * wf[1, l, 16:24]) * north
        return carry

    lax.fori_loop(0, LEVS, fine_rows, 0)
    for message in own + relays:
        arrive(message)
    for copy, goes in started:
        when(goes, copy.wait_send)


COPIES = 27


def exchange(fine, wind, inc, mis):
    return pl.pallas_call(
        exchange_kernel,
        out_shape=(
            pltpu.VMEM((VARS, LEVS, FROWS, FCOLS), F32),
            pltpu.VMEM((2, LEVS, FROWS, FCOLS), F32),
            pltpu.VMEM((VARS, LEVS, FROWS, FCOLS), F32),
            pltpu.VMEM((2, UNITS, 24, 128), F32),
            pltpu.VMEM((5, ROWS, 24, 128), F32),
            pltpu.VMEM((6, ROWS, 24, COLS), F32),
            pltpu.VMEM((2, 8, 24, 128), F32),
            pltpu.VMEM((256, 2 * FCOLS), BF16),
            pltpu.VMEM((512, FCOLS), BF16),
        ),
        in_specs=[HBM] * 4,
        out_specs=(VMEM,) * 9,
        scratch_shapes=[
            pltpu.VMEM((LEVS * FROWS, 128), F32),
            pltpu.VMEM((2, UNITS, LEVS, 128), F32),
            pltpu.VMEM((2, 8, LEVS, 128), F32),
            pltpu.VMEM((2, VARS, LEVS, FCOLS), F32),
            pltpu.VMEM((2, VARS, LEVS, FCOLS), F32),
            pltpu.VMEM((2, VARS, 8, 128), F32),
            pltpu.VMEM((2, VARS, 8, 128), F32),
            pltpu.VMEM((VARS, FROWS, FCOLS), F32),
            pltpu.VMEM((FCOLS, 128), BF16),
            pltpu.SemaphoreType.DMA((7,)),
            pltpu.SemaphoreType.REGULAR,
            pltpu.SemaphoreType.REGULAR,
            pltpu.SemaphoreType.DMA((COPIES,)),
            pltpu.SemaphoreType.DMA((COPIES,)),
        ],
        compiler_params=pltpu.CompilerParams(
            vmem_limit_bytes=20 << 20, collective_id=0, has_side_effects=True
        ),
        name="exchange",
    )(fine, wind, inc, mis)


def solve_kernel(
    fs, wf, base, yp, cwo, imo, xm, table_a, table_b,
    fine_next, gradient,
    q, st, sc, d1, res, a1, up, vr, lv, ly, grad, out, out_sem,
):
    gy, lev = lax.axis_index("gy"), lax.axis_index("lev")
    lane = lax.broadcasted_iota(jnp.int32, (24, 128), 1)
    level = lax.broadcasted_iota(jnp.int32, (24, 128), 0)
    top = jnp.where(lev == 1, 15, 24)
    bottom = jnp.where(lev == 0, 0, 24)
    above = jnp.where(level == top, 0.0, 0.1).astype(F32)
    below = jnp.where(level == bottom, 0.0, 0.1).astype(F32)

    first_row = jnp.where(gy == 0, 5, 0)
    last_row = jnp.where(gy == NGY - 1, 10, 15)

    def within(e):
        return jnp.logical_and(e >= first_row, e <= last_row)

    def inside(e):
        return jnp.where(within(e), 1.0, 0.0).astype(F32)

    def fill(f, e, body, u, at, width):
        left = pltpu.roll(xm[0, u], (128 - width - at) % 128, 1)
        right = pltpu.roll(xm[1, u], (COLS - at) % 128, 1)
        value = jnp.where(lane < COLS, body, jnp.where(lane >= 112, left, right))
        if not 5 <= e < 11:
            value = jnp.where(within(e), value, 0.0)
        q[f, e] = value

    for f in range(FIELDS):
        for j in range(ROWS):
            if f < 5:
                body = cwo[f, j]
            else:
                body = jnp.concatenate([imo[f - 5, j], jnp.zeros((24, 32), F32)], axis=1)
            fill(f, 5 + j, body, j, *SEG_ROW[f])
    for s in range(2):
        for i, (f, k) in enumerate(ITEMS):
            g, m = i // 4, i % 4
            if m < 3:
                body = yp[s, 3 * g + m]
            else:
                pieces = [pltpu.roll(yp[s, 3 * g + n], 32 + 32 * n, 1) for n in range(3)]
                body = jnp.where(
                    lane < 32, pieces[0], jnp.where(lane < 64, pieces[1], pieces[2])
                )
            fill(f, 5 - k if s == 0 else 10 + k, body, 6 + s, *SEG_CORNER[f, k])

    def east(x):
        return pltpu.roll(x, 127, 1)

    def west(x):
        return pltpu.roll(x, 1, 1)

    def vertical(x):
        return pltpu.roll(x, 23, 0) * above + pltpu.roll(x, 1, 0) * below

    def forward(ref, base, v, e, wu, wv):
        k = MIX[v]
        x = ref[base + v, e]
        total = (1.0 - 4.0 * k - 0.2) * x + vertical(x)
        total += (k - wu) * east(x) + (k + wu) * west(x)
        total += (k - wv) * ref[base + v, e + 1] + (k + wv) * ref[base + v, e - 1]
        return x, total

    def adjoint(ref, v, e, wu, wn, ws):
        k = MIX[v]
        x = ref[v, e]
        total = (1.0 - 4.0 * k - 0.2) * x + vertical(x)
        total += east((k + wu) * x) + west((k - wu) * x)
        total += (k + wn) * ref[v, e + 1] + (k - ws) * ref[v, e - 1]
        return x, total

    def slope(x):
        t = jnp.tanh(x)
        return t, 0.3 - 0.3 * t * t

    def winds(e):
        return 0.125 * q[3, e], 0.125 * q[4, e]

    def stage_one(e, carry):
        wu, wv = winds(e)
        keep = inside(e)
        for v in range(VARS):
            _, s = slope(q[v, e])
            sc[v, e] = s
            x, total = forward(q, 5, v, e, wu, wv)
            d1[v, e] = (total - s * x) * keep
        return carry

    for e in range(1, 15):
        stage_one(e, 0)

    def stage_path(e, carry):
        wu, wv = winds(e)
        for v in range(VARS):
            x, total = forward(q, 0, v, e, wu, wv)
            _, s = slope(total - 0.3 * jnp.tanh(x))
            st[v, e] = s
        return carry

    for e in range(2, 14):
        stage_path(e, 0)

    def stage_two(e, carry):
        wu, wv = winds(e)
        keep = inside(e)
        for v in range(VARS):
            x, total = forward(d1, 0, v, e, wu, wv)
            res[v, e] = (total - st[v, e] * x - q[8 + v, e]) * keep
        return carry

    for e in range(2, 14):
        stage_two(e, 0)

    def stage_three(e, carry):
        wu, _ = winds(e)
        keep = inside(e)
        wn, ws = 0.125 * q[4, e + 1], 0.125 * q[4, e - 1]
        for v in range(VARS):
            x, total = adjoint(res, v, e, wu, wn, ws)
            a1[v, e] = (total - st[v, e] * x) * keep
        return carry

    for e in range(3, 13):
        stage_three(e, 0)

    def stage_four(e, carry):
        wu, _ = winds(e)
        keep = inside(e)
        wn, ws = 0.125 * q[4, e + 1], 0.125 * q[4, e - 1]
        for v in range(VARS):
            x, total = adjoint(a1, v, e, wu, wn, ws)
            start = q[5 + v, e]
            slant = start + total - sc[v, e] * x
            up[v, e - 4] = (start - 0.5 * slant) * keep
            q[v, e] = slant
        return carry

    for e in range(4, 12):
        stage_four(e, 0)
    for v in range(VARS):
        for j in range(ROWS):
            grad[v, j] = q[v, 5 + j, 0:16, 0:COLS]
    grad_copy = pltpu.make_async_copy(grad, gradient, out_sem.at[6])
    grad_copy.start()

    pieces = ((0.375, 0.625, 0.0), (0.125, 0.875, 0.0), (0.0, 0.875, 0.125), (0.0, 0.625, 0.375))
    low, high = inside(4), inside(11)
    outs = []
    for v in range(VARS):
        k = MIX[v]
        rows = [up[v, e] for e in range(8)]

        def fine_row(r):
            j, a = r // 4, r % 4
            c = pieces[a]
            value = c[1] * rows[j + 1]
            value += c[0] * rows[j] if c[0] else c[2] * rows[j + 2]
            if r == -1:
                value = value * low
            if r == 24:
                value = value * high
            return value

        south, here = fine_row(-1), fine_row(0)
        for r in range(FROWS):
            north = fine_row(r + 1)
            mixed = ((0.8 - 4.0 * k) / k) * here + (north + south) + (1.0 / k) * vertical(here)
            at = pl.ds(24 * r, LEVS)
            vr[0, at, :] = here[0:16]
            vr[1, at, :] = mixed[0:16]
            vr[2, at, :] = 0.125 * (south - north)[0:16]
            south, here = here, north
        for l in range(LEVS):
            at = pl.ds(24 * l, 24)
            by_level = pl.ds(l, 24, stride=24)
            lv[at, 256:384], lv[at, 384:512] = two_parts(vr[0, by_level, :])
            lv[at, 0:128], lv[at, 128:256] = two_parts(vr[1, by_level, :])
            ly[at, 0:128], ly[at, 128:256] = two_parts(vr[2, by_level, :])
        for c in range(2):
            at = slice(192 * c, 192 * c + 192)
            levels = slice(8 * c, 8 * c + 8)
            shape = (8, FROWS, FCOLS)

            def dot(x, t):
                return jnp.dot(x, t, preferred_element_type=F32).reshape(shape)

            step = dot(lv[at, 256:512], table_a[:, 0:FCOLS])
            total = base[v, levels] - 0.3 * jnp.tanh(fs[v, levels] + step)
            total += k * dot(lv[at, :], table_b[...])
            total += wf[0, levels] * dot(lv[at, 256:512], table_a[:, FCOLS:])
            total += wf[1, levels] * dot(ly[at, :], table_a[:, 0:FCOLS])
            out[v, levels] = total
            copy = pltpu.make_async_copy(
                out.at[v, levels], fine_next.at[v, levels], out_sem.at[2 * v + c]
            )
            copy.start()
            outs.append(copy)
    for copy in outs:
        copy.wait()
    grad_copy.wait()


def solve(*args):
    line = lambda n: pltpu.VMEM((n, 16, 24, 128), F32)
    return pl.pallas_call(
        solve_kernel,
        out_shape=(
            jax.ShapeDtypeStruct((VARS, LEVS, FROWS, FCOLS), F32),
            jax.ShapeDtypeStruct((VARS, ROWS, LEVS, COLS), F32),
        ),
        in_specs=[VMEM] * 9,
        out_specs=(HBM, HBM),
        scratch_shapes=[
            line(FIELDS), line(3), line(3), line(3), line(3), line(3),
            pltpu.VMEM((VARS, 8, 24, 128), F32),
            pltpu.VMEM((3, 24 * 24, 128), F32),
            pltpu.VMEM((LEVS * FROWS, 512), BF16),
            pltpu.VMEM((LEVS * FROWS, 256), BF16),
            pltpu.VMEM((VARS, ROWS, LEVS, COLS), F32),
            pltpu.VMEM((VARS, LEVS, FROWS, FCOLS), F32),
            pltpu.SemaphoreType.DMA((7,)),
        ],
        compiler_params=pltpu.CompilerParams(vmem_limit_bytes=40 << 20),
        name="solve",
    )(*args)


def per_device(fine_state, wind_field, increment, misfit):
    inc = jnp.transpose(increment, (0, 2, 1, 3))
    mis = jnp.transpose(misfit, (0, 2, 1, 3))
    held = [pltpu.with_memory_space_constraint(x, pltpu.HBM) for x in (fine_state, wind_field, inc, mis)]
    fine_next, gradient = solve(*exchange(*held))
    return fine_next, jnp.transpose(gradient, (0, 2, 1, 3))


def solution(mesh):
    spec = P(None, "lev", "gy", "gx")
    return jax.shard_map(
        per_device, mesh=mesh, in_specs=(spec,) * 4, out_specs=(spec, spec), check_vma=False
    )
```

```python
import functools

import jax
import jax.numpy as jnp
from jax import lax
from jax.experimental import pallas as pl
from jax.experimental.pallas import tpu as pltpu
from jax.sharding import PartitionSpec as P

MESH = pl.DeviceIdType.MESH
F32 = jnp.float32
BF16 = jnp.bfloat16
HBM = pl.BlockSpec(memory_space=pltpu.HBM)
VMEM = pl.BlockSpec(memory_space=pltpu.VMEM)

MIX = (0.05, 0.1, 0.2)
VARS, LEVS, ROWS, COLS = 3, 16, 6, 96
FROWS, FCOLS = 24, 384
NGX, NGY = 4, 16

DEPTH = (4, 4, 4, 4, 4, 5, 5, 5, 3, 3, 3)
FIELDS = len(DEPTH)


def segments_row():
    place, at = {}, 0
    for f in range(FIELDS):
        place[f] = (at, DEPTH[f])
        at += DEPTH[f]
    return place


def segments_corner():
    place, at = {}, 0
    for f in range(FIELDS):
        for k in range(1, DEPTH[f] + 1):
            place[f, k] = (at, DEPTH[f] + 1 - k)
            at += DEPTH[f] + 1 - k
    return place


SEG_ROW = segments_row()
SEG_CORNER = segments_corner()


ITEMS = [(f, k) for f in range(5, FIELDS) for k in range(1, DEPTH[f] + 1)]
EARLY = 3 * len(ITEMS) // 4
ITEMS += [(f, k) for f in range(5) for k in range(1, DEPTH[f] + 1)]
UNITS = 3 * len(ITEMS) // 4


def two_parts(x):
    high = x.astype(BF16)
    return high, (x - high.astype(F32)).astype(BF16)


def exchange_kernel(
    fine, wind, inc, mis,
    fs, wf, base, yp, cwo, imo, xm, table_a, table_b,
    half, ys, xs, fys, fy, fxs, fx, fl, table,
    load_sem, answer, known, ready, send_sem, recv_sem,
):
    gx, gy, lev = lax.axis_index("gx"), lax.axis_index("gy"), lax.axis_index("lev")
    gxs = (lax.rem(gx + 1, NGX), lax.rem(gx + NGX - 1, NGX))
    gys = (lax.rem(gy + 1, NGY), lax.rem(gy + NGY - 1, NGY))
    partner = (gx, gy, 1 - lev)
    near = [(gx, gys[0], lev), (gx, gys[1], lev), (gxs[0], gy, lev), (gxs[1], gy, lev)]

    has_next, has_last = gy < NGY - 1, gy > 0
    going, coming = (has_next, has_last), (has_last, has_next)
    rows_near = has_next.astype(jnp.int32) + has_last.astype(jnp.int32)

    def signal(semaphore, device, condition=None):
        def act():
            pl.semaphore_signal(semaphore, inc=1, device_id=device, device_id_type=MESH)

        act() if condition is None else pl.when(condition)(act)

    barrier = pltpu.get_barrier_semaphore()
    for s in range(2):
        signal(barrier, near[s], going[s])
    signal(barrier, partner)
    signal(barrier, near[2], gx < NGX - 1)
    signal(barrier, near[3], gx == 0)
    greeted = (gx > 0).astype(jnp.int32) + (gx == NGX - 1).astype(jnp.int32)
    answered = (gx < NGX - 1).astype(jnp.int32) + (gx == 0).astype(jnp.int32)

    loads = [
        pltpu.make_async_copy(inc, imo.at[0:3, :, 0:16, :], load_sem.at[5]),
        pltpu.make_async_copy(mis, imo.at[3:6, :, 0:16, :], load_sem.at[6]),
    ]
    for f in range(VARS):
        loads.append(pltpu.make_async_copy(fine.at[f], fs.at[f], load_sem.at[f]))
    for f in range(2):
        loads.append(pltpu.make_async_copy(wind.at[f], wf.at[f], load_sem.at[3 + f]))
    for copy in loads:
        copy.start()

    source = lax.broadcasted_iota(jnp.int32, (FCOLS, 128), 0) // 4
    target = lax.broadcasted_iota(jnp.int32, (FCOLS, 128), 1)
    mean = jnp.where(source == target, 0.0625, 0.0).astype(BF16)
    table[0:FCOLS] = mean
    table[FCOLS : 2 * FCOLS] = mean

    started = []

    def when(condition, act):
        act() if condition is None else pl.when(condition)(act)

    def prepare(src, dst, device, goes=None, comes=None):
        i = len(started)
        copy = pltpu.make_async_remote_copy(
            src_ref=src, dst_ref=dst, send_sem=send_sem.at[i], recv_sem=recv_sem.at[i],
            device_id=device, device_id_type=MESH,
        )
        started.append((copy, goes))
        return copy, comes, goes

    def send(*args):
        message = prepare(*args)
        when(message[2], message[0].start)
        return message

    def start(message, condition):
        goes = message[2]
        both = condition if goes is None else jnp.logical_and(condition, goes)
        pl.when(both)(message[0].start)

    def arrive(message):
        when(message[1], message[0].wait_recv)

    def send_row(src, dst, s):
        return send(src, dst, near[s], going[s], coming[s])

    def relay(ref, at, comes=None):
        dst = ref.at[(*at, slice(16, 24), slice(None))]
        return send(ref.at[(*at, tile, slice(None))], dst, partner, comes, comes)

    tile = pl.ds(pl.multiple_of((1 - lev) * 8, 8), 8)
    lane = lax.broadcasted_iota(jnp.int32, (LEVS, 128), 1)

    def unit(f, j):
        if f < 5:
            return cwo[f, j, 0:16, :]
        body = imo[f - 5, j, 0:16, :]
        return jnp.concatenate([body, jnp.zeros((LEVS, 128 - COLS), F32)], axis=1)

    def row_of(s, k):
        return ROWS - k if s == 0 else k - 1

    def pack_rows(s, start, stop):
        for g in range(start // 3, stop // 3):
            parts = [unit(f, row_of(s, k)) for f, k in ITEMS[4 * g : 4 * g + 4]]
            for m in range(3):
                rest = pltpu.roll(parts[3], 96 - 32 * m, 1)
                ys[s, 3 * g + m] = jnp.where(lane < COLS, parts[m], rest)

    loads[0].wait()
    loads[1].wait()
    for s in range(2):
        pack_rows(s, 0, EARLY)
    def coarsen(f):
        loads[2 + f].wait()
        ref = fs[f] if f < VARS else wf[f - VARS]
        parts = jnp.concatenate(two_parts(ref.reshape(LEVS * FROWS, FCOLS)), axis=1)
        half[...] = jnp.dot(parts, table[...], preferred_element_type=F32)
        for j in range(ROWS):
            total = half[pl.ds(4 * j, LEVS, stride=FROWS), :]
            for a in range(1, 4):
                total += half[pl.ds(4 * j + a, LEVS, stride=FROWS), :]
            cwo[f, j, 0:16, :] = total

    coarsen(0)
    coarsen(1)
    pl.semaphore_wait(barrier, rows_near + greeted + 1)
    y_im = [send_row(ys.at[s, 0:EARLY], yp.at[s, 0:EARLY, 0:16, :], s) for s in range(2)]
    signal(answer, near[3], gx > 0)
    signal(answer, near[2], gx == NGX - 1)
    early, late = answered == 0, answered > 0
    signal(known, partner, early)
    own = [send(imo.at[:, :, tile, :], imo.at[:, :, 16:24, :], partner)]

    coarsen(2)
    pl.when(early)(lambda: pl.semaphore_wait(known, 1))
    for s in range(2):
        signal(ready, near[s], jnp.logical_and(going[s], early))
    coarsen(3)
    coarsen(4)
    def packed(out, value, h, at, width):
        first = COLS - width if h == 0 else 0
        moved = pltpu.roll(value, (at - first) % 128, 1)
        return jnp.where(jnp.logical_and(lane >= at, lane < at + width), moved, out)

    zero = jnp.zeros((LEVS, 128), F32)
    for h in range(2):
        for s in range(2):
            out = zero
            for (f, k), (at, width) in SEG_CORNER.items():
                out = packed(out, unit(f, row_of(s, k)), h, at, width)
            xs[h, 6 + s] = out
    def prepare_pair(h, at, device, goes=None, comes=None):
        there = xm.at[h, at]
        spread = (slice(None),) * (len(there.shape) - 2)
        low, adjacent = (*spread, slice(0, 16)), (*spread, slice(16, 24))
        cross = (*device[:2], 1 - lev)
        return [
            prepare(xs.at[h, at], there.at[low], device, goes, comes),
            prepare(xs.at[h, at].at[(*spread, tile)], there.at[adjacent], cross, goes, comes),
        ]

    corner = []
    for h in range(2):
        for s in range(2):
            device = (gxs[h], gys[s], lev)
            corner += prepare_pair(h, 6 + s, device, going[s], coming[s])

    def send_corners(condition):
        pl.when(condition)(lambda: pl.semaphore_wait(ready, rows_near))
        for message in corner:
            start(message, condition)

    send_corners(early)
    for s in range(2):
        pack_rows(s, EARLY, UNITS)
    y_cw = [
        send_row(ys.at[s, EARLY:UNITS], yp.at[s, EARLY:UNITS, 0:16, :], s) for s in range(2)
    ]
    own.append(send(cwo.at[:, :, tile, :], cwo.at[:, :, 16:24, :], partner))

    for h in range(2):
        for j in range(ROWS):
            out = zero
            for f, (at, width) in SEG_ROW.items():
                out = packed(out, unit(f, j), h, at, width)
            xs[h, j] = out
    x_row = []
    for h in range(2):
        x_row += prepare_pair(h, slice(0, 6), near[2 + h])
    for message in x_row:
        start(message, early)
    edge = 15 * (1 - lev)
    fine_lev = send(fs.at[:, edge], fl, partner)

    for v in range(VARS):
        for l in range(LEVS):
            fys[0, v, l : l + 1, :] = fs[v, l, FROWS - 1 : FROWS, :]
            fys[1, v, l : l + 1, :] = fs[v, l, 0:1, :]
    y_fine = [send_row(fys.at[s], fy.at[s], s) for s in range(2)]

    lane8 = lax.broadcasted_iota(jnp.int32, (8, 128), 1)
    for v in range(VARS):
        outs = [jnp.zeros((8, 128), F32)] * 2
        for l in range(LEVS):
            for t in range(3):
                n = 3 * l + t
                first = pltpu.roll(fs[v, l, 8 * t : 8 * t + 8, 0:128], n, 1)
                last = pltpu.roll(fs[v, l, 8 * t : 8 * t + 8, 256:384], (n + 1) % 128, 1)
                outs[0] = jnp.where(lane8 == n, last, outs[0])
                outs[1] = jnp.where(lane8 == n, first, outs[1])
        fxs[0, v] = outs[0]
        fxs[1, v] = outs[1]
    x_fine = [prepare(fxs.at[h], fx.at[h], near[2 + h]) for h in range(2)]
    for message in x_fine:
        start(message, early)

    coarse_lane = lax.broadcasted_iota(jnp.int32, (128, FCOLS), 0)
    fine_col = lax.broadcasted_iota(jnp.int32, (128, FCOLS), 1)

    def columns(shift):
        scaled = 4 * (fine_col + shift) + 10
        beneath = lax.shift_right_arithmetic(scaled, 4)
        fraction = jnp.bitwise_and(scaled, 15).astype(F32) * 0.0625
        first = coarse_lane == jnp.bitwise_and(beneath - 1, 127)
        second = coarse_lane == jnp.bitwise_and(beneath, 127)
        return jnp.where(first, 1.0 - fraction, 0.0) + jnp.where(second, fraction, 0.0)

    middle = columns(0).astype(BF16)
    ahead, behind = columns(1), columns(-1)
    slant = (0.125 * (behind - ahead)).astype(BF16)
    around = (ahead + behind).astype(BF16)
    for part in range(2):
        rows = slice(128 * part, 128 * part + 128)
        table_a[rows, 0:FCOLS] = middle
        table_a[rows, FCOLS:] = slant
        table_b[rows, :] = middle
        table_b[slice(256 + 128 * part, 384 + 128 * part), :] = around

    row = lax.broadcasted_iota(jnp.int32, (FROWS, FCOLS), 0)
    col = lax.broadcasted_iota(jnp.int32, (FROWS, FCOLS), 1)

    def fine_step(l, carry):
        wu, wv = 0.125 * wf[0, l], 0.125 * wf[1, l]
        has_low = jnp.where(l > 0, 0.1, 0.0).astype(F32)
        has_high = jnp.where(l < LEVS - 1, 0.1, 0.0).astype(F32)
        for v in range(VARS):
            k = MIX[v]
            x = fs[v, l]
            total = (1.0 - 4.0 * k - 0.2) * x
            total += has_low * fs[v, jnp.maximum(l - 1, 0)]
            total += has_high * fs[v, jnp.minimum(l + 1, LEVS - 1)]
            total += (k - wu) * jnp.where(col == FCOLS - 1, 0.0, pltpu.roll(x, FCOLS - 1, 1))
            total += (k + wu) * jnp.where(col == 0, 0.0, pltpu.roll(x, 1, 1))
            total += (k - wv) * jnp.where(row == FROWS - 1, 0.0, pltpu.roll(x, FROWS - 1, 0))
            total += (k + wv) * jnp.where(row == 0, 0.0, pltpu.roll(x, 1, 0))
            base[v, l] = total
        return carry

    lax.fori_loop(0, 5, fine_step, 0)
    pl.when(late)(lambda: pl.semaphore_wait(answer, answered))
    signal(known, partner, late)
    pl.when(late)(lambda: pl.semaphore_wait(known, 1))
    for s in range(2):
        signal(ready, near[s], jnp.logical_and(going[s], late))
    for message in x_row + x_fine:
        start(message, late)
    lax.fori_loop(5, 10, fine_step, 0)
    send_corners(late)
    lax.fori_loop(10, LEVS, fine_step, 0)

    relays = []
    for s in range(2):
        arrive(y_im[s])
        relays.append(relay(yp, (s, slice(0, EARLY)), coming[s]))
    for s in range(2):
        arrive(y_cw[s])
        relays.append(relay(yp, (s, slice(EARLY, UNITS)), coming[s]))
    for message in x_fine + [fine_lev]:
        arrive(message)

    def fine_columns(l, carry):
        for v in range(VARS):
            k = MIX[v]
            for t in range(3):
                n = 3 * l + t
                rows = slice(8 * t, 8 * t + 8)
                left = pltpu.roll(fx[0, v], lax.rem(128 - n, 128), 1)
                right = pltpu.roll(fx[1, v], 127 - n, 1)
                wu0, wu1 = 0.125 * wf[0, l, rows, 0:128], 0.125 * wf[0, l, rows, 256:384]
                base[v, l, rows, 0:128] += jnp.where(lane8 == 0, (k + wu0) * left, 0.0)
                base[v, l, rows, 256:384] += jnp.where(lane8 == 127, (k - wu1) * right, 0.0)
        return carry

    lax.fori_loop(0, LEVS, fine_columns, 0)
    for v in range(VARS):
        base[v, edge] += 0.1 * fl[v]

    for message in y_fine:
        arrive(message)
    sub8 = lax.broadcasted_iota(jnp.int32, (8, FCOLS), 0)

    def fine_rows(l, carry):
        for v in range(VARS):
            k = MIX[v]
            south = jnp.broadcast_to(fy[0, v, pl.ds(l, 1), :], (8, FCOLS))
            north = jnp.broadcast_to(fy[1, v, pl.ds(l, 1), :], (8, FCOLS))
            south = jnp.where(jnp.logical_and(sub8 == 0, gy > 0), south, 0.0)
            north = jnp.where(jnp.logical_and(sub8 == 7, gy < NGY - 1), north, 0.0)
            base[v, l, 0:8] += (k + 0.125 * wf[1, l, 0:8]) * south
            base[v, l, 16:24] += (k - 0.125 * wf[1, l, 16:24]) * north
        return carry

    lax.fori_loop(0, LEVS, fine_rows, 0)
    for message in own + relays + x_row + corner:
        arrive(message)
    for copy, goes in started:
        when(goes, copy.wait_send)


COPIES = 27


def exchange(fine, wind, inc, mis):
    return pl.pallas_call(
        exchange_kernel,
        out_shape=(
            pltpu.VMEM((VARS, LEVS, FROWS, FCOLS), F32),
            pltpu.VMEM((2, LEVS, FROWS, FCOLS), F32),
            pltpu.VMEM((VARS, LEVS, FROWS, FCOLS), F32),
            pltpu.VMEM((2, UNITS, 24, 128), F32),
            pltpu.VMEM((5, ROWS, 24, 128), F32),
            pltpu.VMEM((6, ROWS, 24, COLS), F32),
            pltpu.VMEM((2, 8, 24, 128), F32),
            pltpu.VMEM((256, 2 * FCOLS), BF16),
            pltpu.VMEM((512, FCOLS), BF16),
        ),
        in_specs=[HBM] * 4,
        out_specs=(VMEM,) * 9,
        scratch_shapes=[
            pltpu.VMEM((LEVS * FROWS, 128), F32),
            pltpu.VMEM((2, UNITS, LEVS, 128), F32),
            pltpu.VMEM((2, 8, LEVS, 128), F32),
            pltpu.VMEM((2, VARS, LEVS, FCOLS), F32),
            pltpu.VMEM((2, VARS, LEVS, FCOLS), F32),
            pltpu.VMEM((2, VARS, 8, 128), F32),
            pltpu.VMEM((2, VARS, 8, 128), F32),
            pltpu.VMEM((VARS, FROWS, FCOLS), F32),
            pltpu.VMEM((2 * FCOLS, 128), BF16),
            pltpu.SemaphoreType.DMA((7,)),
            pltpu.SemaphoreType.REGULAR,
            pltpu.SemaphoreType.REGULAR,
            pltpu.SemaphoreType.REGULAR,
            pltpu.SemaphoreType.DMA((COPIES,)),
            pltpu.SemaphoreType.DMA((COPIES,)),
        ],
        compiler_params=pltpu.CompilerParams(
            vmem_limit_bytes=20 << 20, collective_id=0, has_side_effects=True
        ),
        name="exchange",
    )(fine, wind, inc, mis)


def solve_kernel(
    fs, wf, base, yp, cwo, imo, xm, table_a, table_b,
    fine_next, gradient,
    q, st, sc, d1, res, a1, up, vr, lv, ly, grad, out, out_sem,
):
    gy, lev = lax.axis_index("gy"), lax.axis_index("lev")
    lane = lax.broadcasted_iota(jnp.int32, (24, 128), 1)
    level = lax.broadcasted_iota(jnp.int32, (24, 128), 0)
    top = jnp.where(lev == 1, 15, 24)
    bottom = jnp.where(lev == 0, 0, 24)
    above = jnp.where(level == top, 0.0, 0.1).astype(F32)
    below = jnp.where(level == bottom, 0.0, 0.1).astype(F32)

    first_row = jnp.where(gy == 0, 5, 0)
    last_row = jnp.where(gy == NGY - 1, 10, 15)

    def within(e):
        return jnp.logical_and(e >= first_row, e <= last_row)

    def inside(e):
        return jnp.where(within(e), 1.0, 0.0).astype(F32)

    def fill(f, e, body, u, at, width):
        left = pltpu.roll(xm[0, u], (128 - width - at) % 128, 1)
        right = pltpu.roll(xm[1, u], (COLS - at) % 128, 1)
        value = jnp.where(lane < COLS, body, jnp.where(lane >= 112, left, right))
        if not 5 <= e < 11:
            value = jnp.where(within(e), value, 0.0)
        q[f, e] = value

    for f in range(FIELDS):
        for j in range(ROWS):
            if f < 5:
                body = cwo[f, j]
            else:
                body = jnp.concatenate([imo[f - 5, j], jnp.zeros((24, 32), F32)], axis=1)
            fill(f, 5 + j, body, j, *SEG_ROW[f])
    for s in range(2):
        for i, (f, k) in enumerate(ITEMS):
            g, m = i // 4, i % 4
            if m < 3:
                body = yp[s, 3 * g + m]
            else:
                pieces = [pltpu.roll(yp[s, 3 * g + n], 32 + 32 * n, 1) for n in range(3)]
                body = jnp.where(
                    lane < 32, pieces[0], jnp.where(lane < 64, pieces[1], pieces[2])
                )
            fill(f, 5 - k if s == 0 else 10 + k, body, 6 + s, *SEG_CORNER[f, k])

    def east(x):
        return pltpu.roll(x, 127, 1)

    def west(x):
        return pltpu.roll(x, 1, 1)

    def vertical(x):
        return pltpu.roll(x, 23, 0) * above + pltpu.roll(x, 1, 0) * below

    def forward(ref, base, v, e, wu, wv):
        k = MIX[v]
        x = ref[base + v, e]
        total = (1.0 - 4.0 * k - 0.2) * x + vertical(x)
        total += (k - wu) * east(x) + (k + wu) * west(x)
        total += (k - wv) * ref[base + v, e + 1] + (k + wv) * ref[base + v, e - 1]
        return x, total

    def adjoint(ref, v, e, wu, wn, ws):
        k = MIX[v]
        x = ref[v, e]
        total = (1.0 - 4.0 * k - 0.2) * x + vertical(x)
        total += east((k + wu) * x) + west((k - wu) * x)
        total += (k + wn) * ref[v, e + 1] + (k - ws) * ref[v, e - 1]
        return x, total

    def slope(x):
        t = jnp.tanh(x)
        return t, 0.3 - 0.3 * t * t

    def winds(e):
        return 0.125 * q[3, e], 0.125 * q[4, e]

    def stage_one(e, carry):
        wu, wv = winds(e)
        keep = inside(e)
        for v in range(VARS):
            _, s = slope(q[v, e])
            sc[v, e] = s
            x, total = forward(q, 5, v, e, wu, wv)
            d1[v, e] = (total - s * x) * keep
        return carry

    for e in range(1, 15):
        stage_one(e, 0)

    def stage_path(e, carry):
        wu, wv = winds(e)
        for v in range(VARS):
            x, total = forward(q, 0, v, e, wu, wv)
            _, s = slope(total - 0.3 * jnp.tanh(x))
            st[v, e] = s
        return carry

    for e in range(2, 14):
        stage_path(e, 0)

    def stage_two(e, carry):
        wu, wv = winds(e)
        keep = inside(e)
        for v in range(VARS):
            x, total = forward(d1, 0, v, e, wu, wv)
            res[v, e] = (total - st[v, e] * x - q[8 + v, e]) * keep
        return carry

    for e in range(2, 14):
        stage_two(e, 0)

    def stage_three(e, carry):
        wu, _ = winds(e)
        keep = inside(e)
        wn, ws = 0.125 * q[4, e + 1], 0.125 * q[4, e - 1]
        for v in range(VARS):
            x, total = adjoint(res, v, e, wu, wn, ws)
            a1[v, e] = (total - st[v, e] * x) * keep
        return carry

    for e in range(3, 13):
        stage_three(e, 0)

    def stage_four(e, carry):
        wu, _ = winds(e)
        keep = inside(e)
        wn, ws = 0.125 * q[4, e + 1], 0.125 * q[4, e - 1]
        for v in range(VARS):
            x, total = adjoint(a1, v, e, wu, wn, ws)
            start = q[5 + v, e]
            slant = start + total - sc[v, e] * x
            up[v, e - 4] = (start - 0.5 * slant) * keep
            q[v, e] = slant
        return carry

    for e in range(4, 12):
        stage_four(e, 0)
    for v in range(VARS):
        for j in range(ROWS):
            grad[v, j] = q[v, 5 + j, 0:16, 0:COLS]
    grad_copy = pltpu.make_async_copy(grad, gradient, out_sem.at[6])
    grad_copy.start()

    pieces = ((0.375, 0.625, 0.0), (0.125, 0.875, 0.0), (0.0, 0.875, 0.125), (0.0, 0.625, 0.375))
    low, high = inside(4), inside(11)
    outs = []
    for v in range(VARS):
        k = MIX[v]
        rows = [up[v, e] for e in range(8)]

        def fine_row(r):
            j, a = r // 4, r % 4
            c = pieces[a]
            value = c[1] * rows[j + 1]
            value += c[0] * rows[j] if c[0] else c[2] * rows[j + 2]
            if r == -1:
                value = value * low
            if r == 24:
                value = value * high
            return value

        south, here = fine_row(-1), fine_row(0)
        for r in range(FROWS):
            north = fine_row(r + 1)
            mixed = ((0.8 - 4.0 * k) / k) * here + (north + south) + (1.0 / k) * vertical(here)
            at = pl.ds(24 * r, LEVS)
            vr[0, at, :] = here[0:16]
            vr[1, at, :] = mixed[0:16]
            vr[2, at, :] = 0.125 * (south - north)[0:16]
            south, here = here, north
        for l in range(LEVS):
            at = pl.ds(24 * l, 24)
            by_level = pl.ds(l, 24, stride=24)
            lv[at, 256:384], lv[at, 384:512] = two_parts(vr[0, by_level, :])
            lv[at, 0:128], lv[at, 128:256] = two_parts(vr[1, by_level, :])
            ly[at, 0:128], ly[at, 128:256] = two_parts(vr[2, by_level, :])
        for c in range(2):
            at = slice(192 * c, 192 * c + 192)
            levels = slice(8 * c, 8 * c + 8)
            shape = (8, FROWS, FCOLS)

            def dot(x, t):
                return jnp.dot(x, t, preferred_element_type=F32).reshape(shape)

            step = dot(lv[at, 256:512], table_a[:, 0:FCOLS])
            total = base[v, levels] - 0.3 * jnp.tanh(fs[v, levels] + step)
            total += k * dot(lv[at, :], table_b[...])
            total += wf[0, levels] * dot(lv[at, 256:512], table_a[:, FCOLS:])
            total += wf[1, levels] * dot(ly[at, :], table_a[:, 0:FCOLS])
            out[v, levels] = total
            copy = pltpu.make_async_copy(
                out.at[v, levels], fine_next.at[v, levels], out_sem.at[2 * v + c]
            )
            copy.start()
            outs.append(copy)
    for copy in outs:
        copy.wait()
    grad_copy.wait()


def solve(*args):
    line = lambda n: pltpu.VMEM((n, 16, 24, 128), F32)
    return pl.pallas_call(
        solve_kernel,
        out_shape=(
            jax.ShapeDtypeStruct((VARS, LEVS, FROWS, FCOLS), F32),
            jax.ShapeDtypeStruct((VARS, ROWS, LEVS, COLS), F32),
        ),
        in_specs=[VMEM] * 9,
        out_specs=(HBM, HBM),
        scratch_shapes=[
            line(FIELDS), line(3), line(3), line(3), line(3), line(3),
            pltpu.VMEM((VARS, 8, 24, 128), F32),
            pltpu.VMEM((3, 24 * 24, 128), F32),
            pltpu.VMEM((LEVS * FROWS, 512), BF16),
            pltpu.VMEM((LEVS * FROWS, 256), BF16),
            pltpu.VMEM((VARS, ROWS, LEVS, COLS), F32),
            pltpu.VMEM((VARS, LEVS, FROWS, FCOLS), F32),
            pltpu.SemaphoreType.DMA((7,)),
        ],
        compiler_params=pltpu.CompilerParams(vmem_limit_bytes=40 << 20),
        name="solve",
    )(*args)


def per_device(fine_state, wind_field, increment, misfit):
    inc = jnp.transpose(increment, (0, 2, 1, 3))
    mis = jnp.transpose(misfit, (0, 2, 1, 3))
    held = [pltpu.with_memory_space_constraint(x, pltpu.HBM) for x in (fine_state, wind_field, inc, mis)]
    fine_next, gradient = solve(*exchange(*held))
    return fine_next, jnp.transpose(gradient, (0, 2, 1, 3))


def solution(mesh):
    spec = P(None, "lev", "gy", "gx")
    return jax.shard_map(
        per_device, mesh=mesh, in_specs=(spec,) * 4, out_specs=(spec, spec), check_vma=False
    )
```

```python
import functools

import jax
import jax.numpy as jnp
from jax import lax
from jax.experimental import pallas as pl
from jax.experimental.pallas import tpu as pltpu
from jax.sharding import PartitionSpec as P

MESH = pl.DeviceIdType.MESH
F32 = jnp.float32
BF16 = jnp.bfloat16
HBM = pl.BlockSpec(memory_space=pltpu.HBM)
VMEM = pl.BlockSpec(memory_space=pltpu.VMEM)

MIX = (0.05, 0.1, 0.2)
VARS, LEVS, ROWS, COLS = 3, 16, 6, 96
FROWS, FCOLS = 24, 384
NGX, NGY = 4, 16

DEPTH = (4, 4, 4, 4, 4, 5, 5, 5, 3, 3, 3)
FIELDS = len(DEPTH)


def segments_row():
    place, at = {}, 0
    for f in range(FIELDS):
        place[f] = (at, DEPTH[f])
        at += DEPTH[f]
    return place


def segments_corner():
    place, at = {}, 0
    for f in range(FIELDS):
        for k in range(1, DEPTH[f] + 1):
            place[f, k] = (at, DEPTH[f] + 1 - k)
            at += DEPTH[f] + 1 - k
    return place


SEG_ROW = segments_row()
SEG_CORNER = segments_corner()


ITEMS = [(f, k) for f in range(5, FIELDS) for k in range(1, DEPTH[f] + 1)]
EARLY = 3 * len(ITEMS) // 4
ITEMS += [(f, k) for f in range(5) for k in range(1, DEPTH[f] + 1)]
UNITS = 3 * len(ITEMS) // 4


def two_parts(x):
    high = x.astype(BF16)
    return high, (x - high.astype(F32)).astype(BF16)


def exchange_kernel(
    fine, wind, inc, mis,
    fs, wf, base, yp, cwo, imo, xm, table_a, table_b,
    half, ys, xs, fys, fy, fxs, fx, fl, table,
    load_sem, answer, known, ready, send_sem, recv_sem,
):
    gx, gy, lev = lax.axis_index("gx"), lax.axis_index("gy"), lax.axis_index("lev")
    gxs = (lax.rem(gx + 1, NGX), lax.rem(gx + NGX - 1, NGX))
    gys = (lax.rem(gy + 1, NGY), lax.rem(gy + NGY - 1, NGY))
    partner = (gx, gy, 1 - lev)
    near = [(gx, gys[0], lev), (gx, gys[1], lev), (gxs[0], gy, lev), (gxs[1], gy, lev)]

    has_next, has_last = gy < NGY - 1, gy > 0
    going, coming = (has_next, has_last), (has_last, has_next)
    rows_near = has_next.astype(jnp.int32) + has_last.astype(jnp.int32)

    def signal(semaphore, device, condition=None):
        def act():
            pl.semaphore_signal(semaphore, inc=1, device_id=device, device_id_type=MESH)

        act() if condition is None else pl.when(condition)(act)

    barrier = pltpu.get_barrier_semaphore()
    for s in range(2):
        signal(barrier, near[s], going[s])
    signal(barrier, partner)
    signal(barrier, near[2], gx < NGX - 1)
    signal(barrier, near[3], gx == 0)
    greeted = (gx > 0).astype(jnp.int32) + (gx == NGX - 1).astype(jnp.int32)
    answered = (gx < NGX - 1).astype(jnp.int32) + (gx == 0).astype(jnp.int32)

    loads = [
        pltpu.make_async_copy(inc, imo.at[0:3, :, 0:16, :], load_sem.at[5]),
        pltpu.make_async_copy(mis, imo.at[3:6, :, 0:16, :], load_sem.at[6]),
    ]
    for f in range(VARS):
        loads.append(pltpu.make_async_copy(fine.at[f], fs.at[f], load_sem.at[f]))
    for f in range(2):
        loads.append(pltpu.make_async_copy(wind.at[f], wf.at[f], load_sem.at[3 + f]))
    for copy in loads:
        copy.start()

    source = lax.broadcasted_iota(jnp.int32, (FCOLS, 128), 0) // 4
    target = lax.broadcasted_iota(jnp.int32, (FCOLS, 128), 1)
    mean = jnp.where(source == target, 0.0625, 0.0).astype(BF16)
    table[0:FCOLS] = mean
    table[FCOLS : 2 * FCOLS] = mean

    started = []

    def when(condition, act):
        act() if condition is None else pl.when(condition)(act)

    def prepare(src, dst, device, goes=None, comes=None):
        i = len(started)
        copy = pltpu.make_async_remote_copy(
            src_ref=src, dst_ref=dst, send_sem=send_sem.at[i], recv_sem=recv_sem.at[i],
            device_id=device, device_id_type=MESH,
        )
        started.append((copy, goes))
        return copy, comes, goes

    def send(*args):
        message = prepare(*args)
        when(message[2], message[0].start)
        return message

    def start(message, condition):
        goes = message[2]
        both = condition if goes is None else jnp.logical_and(condition, goes)
        pl.when(both)(message[0].start)

    def arrive(message):
        when(message[1], message[0].wait_recv)

    def send_row(src, dst, s):
        return send(src, dst, near[s], going[s], coming[s])

    def relay(ref, at, comes=None):
        dst = ref.at[(*at, slice(16, 24), slice(None))]
        return send(ref.at[(*at, tile, slice(None))], dst, partner, comes, comes)

    tile = pl.ds(pl.multiple_of((1 - lev) * 8, 8), 8)
    lane = lax.broadcasted_iota(jnp.int32, (LEVS, 128), 1)

    def unit(f, j):
        if f < 5:
            return cwo[f, j, 0:16, :]
        body = imo[f - 5, j, 0:16, :]
        return jnp.concatenate([body, jnp.zeros((LEVS, 128 - COLS), F32)], axis=1)

    def row_of(s, k):
        return ROWS - k if s == 0 else k - 1

    def pack_rows(s, start, stop):
        for g in range(start // 3, stop // 3):
            parts = [unit(f, row_of(s, k)) for f, k in ITEMS[4 * g : 4 * g + 4]]
            for m in range(3):
                rest = pltpu.roll(parts[3], 96 - 32 * m, 1)
                ys[s, 3 * g + m] = jnp.where(lane < COLS, parts[m], rest)

    loads[0].wait()
    loads[1].wait()
    for s in range(2):
        pack_rows(s, 0, EARLY)
    def coarsen(f):
        loads[2 + f].wait()
        ref = fs[f] if f < VARS else wf[f - VARS]
        parts = jnp.concatenate(two_parts(ref.reshape(LEVS * FROWS, FCOLS)), axis=1)
        half[...] = jnp.dot(parts, table[...], preferred_element_type=F32)
        for j in range(ROWS):
            total = half[pl.ds(4 * j, LEVS, stride=FROWS), :]
            for a in range(1, 4):
                total += half[pl.ds(4 * j + a, LEVS, stride=FROWS), :]
            cwo[f, j, 0:16, :] = total

    coarsen(0)
    coarsen(1)
    pl.semaphore_wait(barrier, rows_near + greeted + 1)
    y_im = [send_row(ys.at[s, 0:EARLY], yp.at[s, 0:EARLY, 0:16, :], s) for s in range(2)]
    signal(answer, near[3], gx > 0)
    signal(answer, near[2], gx == NGX - 1)
    early, late = answered == 0, answered > 0
    between, lowest = jnp.logical_and(late, gx > 0), gx == 0
    signal(known, partner, early)
    own = [send(imo.at[:, :, tile, :], imo.at[:, :, 16:24, :], partner)]

    coarsen(2)
    pl.when(early)(lambda: pl.semaphore_wait(known, 1))
    for s in range(2):
        signal(ready, near[s], jnp.logical_and(going[s], early))
    coarsen(3)
    coarsen(4)
    def packed(out, value, h, at, width):
        first = COLS - width if h == 0 else 0
        moved = pltpu.roll(value, (at - first) % 128, 1)
        return jnp.where(jnp.logical_and(lane >= at, lane < at + width), moved, out)

    zero = jnp.zeros((LEVS, 128), F32)
    for h in range(2):
        for s in range(2):
            out = zero
            for (f, k), (at, width) in SEG_CORNER.items():
                out = packed(out, unit(f, row_of(s, k)), h, at, width)
            xs[h, 6 + s] = out
    def prepare_pair(h, at, device, goes=None, comes=None):
        there = xm.at[h, at]
        spread = (slice(None),) * (len(there.shape) - 2)
        low, adjacent = (*spread, slice(0, 16)), (*spread, slice(16, 24))
        cross = (*device[:2], 1 - lev)
        return [
            prepare(xs.at[h, at], there.at[low], device, goes, comes),
            prepare(xs.at[h, at].at[(*spread, tile)], there.at[adjacent], cross, goes, comes),
        ]

    corner = []
    for h in range(2):
        for s in range(2):
            device = (gxs[h], gys[s], lev)
            corner += prepare_pair(h, 6 + s, device, going[s], coming[s])

    def send_corners(condition):
        pl.when(condition)(lambda: pl.semaphore_wait(ready, rows_near))
        for message in corner:
            start(message, condition)

    send_corners(early)

    def hear(condition):
        pl.when(condition)(lambda: pl.semaphore_wait(answer, answered))
        signal(known, partner, condition)
        pl.when(condition)(lambda: pl.semaphore_wait(known, 1))
        for s in range(2):
            signal(ready, near[s], jnp.logical_and(going[s], condition))

    for s in range(2):
        pack_rows(s, EARLY, UNITS)
    y_cw = [
        send_row(ys.at[s, EARLY:UNITS], yp.at[s, EARLY:UNITS, 0:16, :], s) for s in range(2)
    ]
    own.append(send(cwo.at[:, :, tile, :], cwo.at[:, :, 16:24, :], partner))

    for h in range(2):
        for j in range(ROWS):
            out = zero
            for f, (at, width) in SEG_ROW.items():
                out = packed(out, unit(f, j), h, at, width)
            xs[h, j] = out
    x_row = []
    for h in range(2):
        x_row += prepare_pair(h, slice(0, 6), near[2 + h])
    hear(between)
    for message in x_row:
        start(message, gx > 0)
    edge = 15 * (1 - lev)
    fine_lev = send(fs.at[:, edge], fl, partner)

    for v in range(VARS):
        for l in range(LEVS):
            fys[0, v, l : l + 1, :] = fs[v, l, FROWS - 1 : FROWS, :]
            fys[1, v, l : l + 1, :] = fs[v, l, 0:1, :]
    y_fine = [
        prepare(fys.at[s], fy.at[s], near[s], going[s], coming[s]) for s in range(2)
    ]
    for message in y_fine:
        start(message, jnp.logical_or(early, lowest))

    lane8 = lax.broadcasted_iota(jnp.int32, (8, 128), 1)
    for v in range(VARS):
        outs = [jnp.zeros((8, 128), F32)] * 2
        for l in range(LEVS):
            for t in range(3):
                n = 3 * l + t
                first = pltpu.roll(fs[v, l, 8 * t : 8 * t + 8, 0:128], n, 1)
                last = pltpu.roll(fs[v, l, 8 * t : 8 * t + 8, 256:384], (n + 1) % 128, 1)
                outs[0] = jnp.where(lane8 == n, last, outs[0])
                outs[1] = jnp.where(lane8 == n, first, outs[1])
        fxs[0, v] = outs[0]
        fxs[1, v] = outs[1]
    x_fine = [prepare(fxs.at[h], fx.at[h], near[2 + h]) for h in range(2)]
    for message in x_fine:
        start(message, gx > 0)

    coarse_lane = lax.broadcasted_iota(jnp.int32, (128, FCOLS), 0)
    fine_col = lax.broadcasted_iota(jnp.int32, (128, FCOLS), 1)

    def columns(shift):
        scaled = 4 * (fine_col + shift) + 10
        beneath = lax.shift_right_arithmetic(scaled, 4)
        fraction = jnp.bitwise_and(scaled, 15).astype(F32) * 0.0625
        first = coarse_lane == jnp.bitwise_and(beneath - 1, 127)
        second = coarse_lane == jnp.bitwise_and(beneath, 127)
        return jnp.where(first, 1.0 - fraction, 0.0) + jnp.where(second, fraction, 0.0)

    middle = columns(0).astype(BF16)
    ahead, behind = columns(1), columns(-1)
    slant = (0.125 * (behind - ahead)).astype(BF16)
    around = (ahead + behind).astype(BF16)
    for part in range(2):
        rows = slice(128 * part, 128 * part + 128)
        table_a[rows, 0:FCOLS] = middle
        table_a[rows, FCOLS:] = slant
        table_b[rows, :] = middle
        table_b[slice(256 + 128 * part, 384 + 128 * part), :] = around

    row = lax.broadcasted_iota(jnp.int32, (FROWS, FCOLS), 0)
    col = lax.broadcasted_iota(jnp.int32, (FROWS, FCOLS), 1)

    def fine_step(l, carry):
        wu, wv = 0.125 * wf[0, l], 0.125 * wf[1, l]
        has_low = jnp.where(l > 0, 0.1, 0.0).astype(F32)
        has_high = jnp.where(l < LEVS - 1, 0.1, 0.0).astype(F32)
        for v in range(VARS):
            k = MIX[v]
            x = fs[v, l]
            total = (1.0 - 4.0 * k - 0.2) * x
            total += has_low * fs[v, jnp.maximum(l - 1, 0)]
            total += has_high * fs[v, jnp.minimum(l + 1, LEVS - 1)]
            total += (k - wu) * jnp.where(col == FCOLS - 1, 0.0, pltpu.roll(x, FCOLS - 1, 1))
            total += (k + wu) * jnp.where(col == 0, 0.0, pltpu.roll(x, 1, 1))
            total += (k - wv) * jnp.where(row == FROWS - 1, 0.0, pltpu.roll(x, FROWS - 1, 0))
            total += (k + wv) * jnp.where(row == 0, 0.0, pltpu.roll(x, 1, 0))
            base[v, l] = total
        return carry

    lax.fori_loop(0, 3, fine_step, 0)
    send_corners(between)
    for message in y_fine:
        start(message, between)
    lax.fori_loop(3, 10, fine_step, 0)
    hear(lowest)
    for message in x_row + x_fine:
        start(message, lowest)
    lax.fori_loop(10, LEVS, fine_step, 0)
    send_corners(lowest)

    relays = []
    for s in range(2):
        arrive(y_im[s])
        relays.append(relay(yp, (s, slice(0, EARLY)), coming[s]))
    for s in range(2):
        arrive(y_cw[s])
        relays.append(relay(yp, (s, slice(EARLY, UNITS)), coming[s]))
    for message in x_fine + [fine_lev]:
        arrive(message)

    def fine_columns(l, carry):
        for v in range(VARS):
            k = MIX[v]
            for t in range(3):
                n = 3 * l + t
                rows = slice(8 * t, 8 * t + 8)
                left = pltpu.roll(fx[0, v], lax.rem(128 - n, 128), 1)
                right = pltpu.roll(fx[1, v], 127 - n, 1)
                wu0, wu1 = 0.125 * wf[0, l, rows, 0:128], 0.125 * wf[0, l, rows, 256:384]
                base[v, l, rows, 0:128] += jnp.where(lane8 == 0, (k + wu0) * left, 0.0)
                base[v, l, rows, 256:384] += jnp.where(lane8 == 127, (k - wu1) * right, 0.0)
        return carry

    lax.fori_loop(0, LEVS, fine_columns, 0)
    for v in range(VARS):
        base[v, edge] += 0.1 * fl[v]

    for message in y_fine:
        arrive(message)
    sub8 = lax.broadcasted_iota(jnp.int32, (8, FCOLS), 0)

    def fine_rows(l, carry):
        for v in range(VARS):
            k = MIX[v]
            south = jnp.broadcast_to(fy[0, v, pl.ds(l, 1), :], (8, FCOLS))
            north = jnp.broadcast_to(fy[1, v, pl.ds(l, 1), :], (8, FCOLS))
            south = jnp.where(jnp.logical_and(sub8 == 0, gy > 0), south, 0.0)
            north = jnp.where(jnp.logical_and(sub8 == 7, gy < NGY - 1), north, 0.0)
            base[v, l, 0:8] += (k + 0.125 * wf[1, l, 0:8]) * south
            base[v, l, 16:24] += (k - 0.125 * wf[1, l, 16:24]) * north
        return carry

    lax.fori_loop(0, LEVS, fine_rows, 0)
    for message in own + relays + x_row + corner:
        arrive(message)
    for copy, goes in started:
        when(goes, copy.wait_send)


COPIES = 27


def exchange(fine, wind, inc, mis):
    return pl.pallas_call(
        exchange_kernel,
        out_shape=(
            pltpu.VMEM((VARS, LEVS, FROWS, FCOLS), F32),
            pltpu.VMEM((2, LEVS, FROWS, FCOLS), F32),
            pltpu.VMEM((VARS, LEVS, FROWS, FCOLS), F32),
            pltpu.VMEM((2, UNITS, 24, 128), F32),
            pltpu.VMEM((5, ROWS, 24, 128), F32),
            pltpu.VMEM((6, ROWS, 24, COLS), F32),
            pltpu.VMEM((2, 8, 24, 128), F32),
            pltpu.VMEM((256, 2 * FCOLS), BF16),
            pltpu.VMEM((512, FCOLS), BF16),
        ),
        in_specs=[HBM] * 4,
        out_specs=(VMEM,) * 9,
        scratch_shapes=[
            pltpu.VMEM((LEVS * FROWS, 128), F32),
            pltpu.VMEM((2, UNITS, LEVS, 128), F32),
            pltpu.VMEM((2, 8, LEVS, 128), F32),
            pltpu.VMEM((2, VARS, LEVS, FCOLS), F32),
            pltpu.VMEM((2, VARS, LEVS, FCOLS), F32),
            pltpu.VMEM((2, VARS, 8, 128), F32),
            pltpu.VMEM((2, VARS, 8, 128), F32),
            pltpu.VMEM((VARS, FROWS, FCOLS), F32),
            pltpu.VMEM((2 * FCOLS, 128), BF16),
            pltpu.SemaphoreType.DMA((7,)),
            pltpu.SemaphoreType.REGULAR,
            pltpu.SemaphoreType.REGULAR,
            pltpu.SemaphoreType.REGULAR,
            pltpu.SemaphoreType.DMA((COPIES,)),
            pltpu.SemaphoreType.DMA((COPIES,)),
        ],
        compiler_params=pltpu.CompilerParams(
            vmem_limit_bytes=20 << 20, collective_id=0, has_side_effects=True
        ),
        name="exchange",
    )(fine, wind, inc, mis)


def solve_kernel(
    fs, wf, base, yp, cwo, imo, xm, table_a, table_b,
    fine_next, gradient,
    q, st, sc, d1, res, a1, up, vr, lv, ly, grad, out, out_sem,
):
    gy, lev = lax.axis_index("gy"), lax.axis_index("lev")
    lane = lax.broadcasted_iota(jnp.int32, (24, 128), 1)
    level = lax.broadcasted_iota(jnp.int32, (24, 128), 0)
    top = jnp.where(lev == 1, 15, 24)
    bottom = jnp.where(lev == 0, 0, 24)
    above = jnp.where(level == top, 0.0, 0.1).astype(F32)
    below = jnp.where(level == bottom, 0.0, 0.1).astype(F32)

    first_row = jnp.where(gy == 0, 5, 0)
    last_row = jnp.where(gy == NGY - 1, 10, 15)

    def within(e):
        return jnp.logical_and(e >= first_row, e <= last_row)

    def inside(e):
        return jnp.where(within(e), 1.0, 0.0).astype(F32)

    def kept(value, e):
        return value if 5 <= e < 11 else value * inside(e)

    def fill(f, e, body, u, at, width):
        left = pltpu.roll(xm[0, u], (128 - width - at) % 128, 1)
        right = pltpu.roll(xm[1, u], (COLS - at) % 128, 1)
        value = jnp.where(lane < COLS, body, jnp.where(lane >= 112, left, right))
        if not 5 <= e < 11:
            value = jnp.where(within(e), value, 0.0)
        if f in (3, 4):
            value = 0.125 * value
        q[f, e] = value

    places = {}
    for s in range(2):
        for i, (f, k) in enumerate(ITEMS):
            places[f, 5 - k if s == 0 else 10 + k] = (s, i // 4, i % 4, k)

    def fill_row(fields, e):
        for f in fields:
            if 5 <= e < 11:
                if f < 5:
                    body = cwo[f, e - 5]
                else:
                    side = jnp.zeros((24, 128 - COLS), F32)
                    body = jnp.concatenate([imo[f - 5, e - 5], side], axis=1)
                fill(f, e, body, e - 5, *SEG_ROW[f])
            elif (f, e) in places:
                s, g, m, k = places[f, e]
                if m < 3:
                    body = yp[s, 3 * g + m]
                else:
                    third = [pltpu.roll(yp[s, 3 * g + n], 32 + 32 * n, 1) for n in range(3)]
                    body = jnp.where(lane < 32, third[0], jnp.where(lane < 64, third[1], third[2]))
                fill(f, e, body, 6 + s, *SEG_CORNER[f, k])

    def east(x):
        return pltpu.roll(x, 127, 1)

    def west(x):
        return pltpu.roll(x, 1, 1)

    def vertical(x):
        return pltpu.roll(x, 23, 0) * above + pltpu.roll(x, 1, 0) * below

    def adjoint(ref, v, e, wu, wn, ws):
        k = MIX[v]
        x = ref[v, e]
        total = (1.0 - 4.0 * k - 0.2) * x + vertical(x)
        total += east((k + wu) * x) + west((k - wu) * x)
        total += (k + wn) * ref[v, e + 1] + (k - ws) * ref[v, e - 1]
        return x, total

    def winds(e):
        return q[3, e], q[4, e]

    def weights(v, wu, wv):
        k = MIX[v]
        return k - wu, k + wu, k - wv, k + wv

    def centre(v, x):
        return (0.8 - 4.0 * MIX[v]) * x + vertical(x)

    def forward(ref, base, v, e, coefficients):
        to_east, to_west, to_north, to_south = coefficients
        x = ref[base + v, e]
        total = centre(v, x) + to_east * east(x) + to_west * west(x)
        total += to_north * ref[base + v, e + 1] + to_south * ref[base + v, e - 1]
        return x, total

    def stage_one(e, carry):
        wu, wv = winds(e)
        for v in range(VARS):
            coefficients = weights(v, wu, wv)
            t = jnp.tanh(q[v, e])
            s = 0.3 - 0.3 * t * t
            if 4 <= e < 12:
                sc[v, e] = s
            x, total = forward(q, 5, v, e, coefficients)
            d1[v, e] = kept(total - s * x, e)
            if 2 <= e < 14:
                _, total = forward(q, 0, v, e, coefficients)
                t = jnp.tanh(total - 0.3 * t)
                st[v, e] = 0.3 - 0.3 * t * t
        return carry


    def stage_two(e, carry):
        wu, wv = winds(e)
        for v in range(VARS):
            x, total = forward(d1, 0, v, e, weights(v, wu, wv))
            res[v, e] = kept(total - st[v, e] * x - q[8 + v, e], e)
        return carry


    def stage_three(e, carry):
        wu, _ = winds(e)
        wn, ws = q[4, e + 1], q[4, e - 1]
        for v in range(VARS):
            x, total = adjoint(res, v, e, wu, wn, ws)
            a1[v, e] = kept(total - st[v, e] * x, e)
        return carry


    def stage_four(e, carry):
        wu, _ = winds(e)
        wn, ws = q[4, e + 1], q[4, e - 1]
        for v in range(VARS):
            x, total = adjoint(a1, v, e, wu, wn, ws)
            start = q[5 + v, e]
            slant = start + total - sc[v, e] * x
            up[v, e - 4] = kept(start - 0.5 * slant, e)
            if 5 <= e < 11:
                grad[v, e - 5] = slant[0:16, 0:COLS]
        return carry

    for front in range(16 + 4):
        if front < 16:
            fill_row(range(8), front)
        e = front - 1
        if 1 <= e < 15:
            stage_one(e, 0)
        e = front - 2
        if 2 <= e < 14:
            fill_row(range(8, 11), e)
            stage_two(e, 0)
        e = front - 3
        if 3 <= e < 13:
            stage_three(e, 0)
        e = front - 4
        if 4 <= e < 12:
            stage_four(e, 0)

    grad_copy = pltpu.make_async_copy(grad, gradient, out_sem.at[6])
    grad_copy.start()

    pieces = ((0.375, 0.625, 0.0), (0.125, 0.875, 0.0), (0.0, 0.875, 0.125), (0.0, 0.625, 0.375))
    low, high = inside(4), inside(11)
    outs = []
    for v in range(VARS):
        k = MIX[v]
        rows = [up[v, e] for e in range(8)]

        def fine_row(r):
            j, a = r // 4, r % 4
            c = pieces[a]
            value = c[1] * rows[j + 1]
            value += c[0] * rows[j] if c[0] else c[2] * rows[j + 2]
            if r == -1:
                value = value * low
            if r == 24:
                value = value * high
            return value

        south, here = fine_row(-1), fine_row(0)
        for r in range(FROWS):
            north = fine_row(r + 1)
            mixed = ((0.8 - 4.0 * k) / k) * here + (north + south) + (1.0 / k) * vertical(here)
            at = pl.ds(24 * r, LEVS)
            vr[0, at, :] = here[0:16]
            vr[1, at, :] = mixed[0:16]
            vr[2, at, :] = 0.125 * (south - north)[0:16]
            south, here = here, north
        for l in range(0, LEVS, 2):
            at = pl.ds(24 * l, 48)

            def pair(i):
                one, two = vr[i, pl.ds(l, 24, stride=24), :], vr[i, pl.ds(l + 1, 24, stride=24), :]
                return two_parts(jnp.concatenate([one, two], axis=0))

            lv[at, 256:384], lv[at, 384:512] = pair(0)
            lv[at, 0:128], lv[at, 128:256] = pair(1)
            ly[at, 0:128], ly[at, 128:256] = pair(2)
        for c in range(2):
            at = slice(192 * c, 192 * c + 192)
            levels = slice(8 * c, 8 * c + 8)
            shape = (8, FROWS, FCOLS)

            def dot(x, t):
                return jnp.dot(x, t, preferred_element_type=F32).reshape(shape)

            both = jnp.dot(lv[at, 256:512], table_a[...], preferred_element_type=F32)
            step = both[:, 0:FCOLS].reshape(shape)
            total = base[v, levels] - 0.3 * jnp.tanh(fs[v, levels] + step)
            total += wf[0, levels] * both[:, FCOLS:].reshape(shape)
            total += k * dot(lv[at, :], table_b[...])
            total += wf[1, levels] * dot(ly[at, :], table_a[:, 0:FCOLS])
            out[v, levels] = total
            copy = pltpu.make_async_copy(
                out.at[v, levels], fine_next.at[v, levels], out_sem.at[2 * v + c]
            )
            copy.start()
            outs.append(copy)
    for copy in outs:
        copy.wait()
    grad_copy.wait()


def solve(*args):
    line = lambda n: pltpu.VMEM((n, 16, 24, 128), F32)
    return pl.pallas_call(
        solve_kernel,
        out_shape=(
            jax.ShapeDtypeStruct((VARS, LEVS, FROWS, FCOLS), F32),
            jax.ShapeDtypeStruct((VARS, ROWS, LEVS, COLS), F32),
        ),
        in_specs=[VMEM] * 9,
        out_specs=(HBM, HBM),
        scratch_shapes=[
            line(FIELDS), line(3), line(3), line(3), line(3), line(3),
            pltpu.VMEM((VARS, 8, 24, 128), F32),
            pltpu.VMEM((3, 24 * 24, 128), F32),
            pltpu.VMEM((LEVS * FROWS, 512), BF16),
            pltpu.VMEM((LEVS * FROWS, 256), BF16),
            pltpu.VMEM((VARS, ROWS, LEVS, COLS), F32),
            pltpu.VMEM((VARS, LEVS, FROWS, FCOLS), F32),
            pltpu.SemaphoreType.DMA((7,)),
        ],
        compiler_params=pltpu.CompilerParams(vmem_limit_bytes=40 << 20),
        name="solve",
    )(*args)


def per_device(fine_state, wind_field, increment, misfit):
    inc = jnp.transpose(increment, (0, 2, 1, 3))
    mis = jnp.transpose(misfit, (0, 2, 1, 3))
    held = [pltpu.with_memory_space_constraint(x, pltpu.HBM) for x in (fine_state, wind_field, inc, mis)]
    fine_next, gradient = solve(*exchange(*held))
    return fine_next, jnp.transpose(gradient, (0, 2, 1, 3))


def solution(mesh):
    spec = P(None, "lev", "gy", "gx")
    return jax.shard_map(
        per_device, mesh=mesh, in_specs=(spec,) * 4, out_specs=(spec, spec), check_vma=False
    )
```

```python
import functools

import jax
import jax.numpy as jnp
from jax import lax
from jax.experimental import pallas as pl
from jax.experimental.pallas import tpu as pltpu
from jax.sharding import PartitionSpec as P

MESH = pl.DeviceIdType.MESH
F32 = jnp.float32
BF16 = jnp.bfloat16
HBM = pl.BlockSpec(memory_space=pltpu.HBM)
VMEM = pl.BlockSpec(memory_space=pltpu.VMEM)

MIX = (0.05, 0.1, 0.2)
VARS, LEVS, ROWS, COLS = 3, 16, 6, 96
FROWS, FCOLS = 24, 384
NGX, NGY = 4, 16

DEPTH = (4, 4, 4, 4, 4, 5, 5, 5, 3, 3, 3)
FIELDS = len(DEPTH)


def segments_row():
    place, at = {}, 0
    for f in range(FIELDS):
        place[f] = (at, DEPTH[f])
        at += DEPTH[f]
    return place


def segments_corner():
    place, at = {}, 0
    for f in range(FIELDS):
        for k in range(1, DEPTH[f] + 1):
            place[f, k] = (at, DEPTH[f] + 1 - k)
            at += DEPTH[f] + 1 - k
    return place


SEG_ROW = segments_row()
SEG_CORNER = segments_corner()


ITEMS = [(f, k) for f in range(5, FIELDS) for k in range(1, DEPTH[f] + 1)]
EARLY = 3 * len(ITEMS) // 4
ITEMS += [(f, k) for f in range(5) for k in range(1, DEPTH[f] + 1)]
UNITS = 3 * len(ITEMS) // 4


def two_parts(x):
    high = x.astype(BF16)
    return high, (x - high.astype(F32)).astype(BF16)


def exchange_kernel(
    fine, wind, inc, mis,
    fs, wf, base, yp, cwo, imo, xm, table_a, table_b,
    half, ys, xs, fys, fy, fxs, fx, fl, table,
    load_sem, answer, known, ready, send_sem, recv_sem,
):
    gx, gy, lev = lax.axis_index("gx"), lax.axis_index("gy"), lax.axis_index("lev")
    gxs = (lax.rem(gx + 1, NGX), lax.rem(gx + NGX - 1, NGX))
    gys = (lax.rem(gy + 1, NGY), lax.rem(gy + NGY - 1, NGY))
    partner = (gx, gy, 1 - lev)
    near = [(gx, gys[0], lev), (gx, gys[1], lev), (gxs[0], gy, lev), (gxs[1], gy, lev)]

    has_next, has_last = gy < NGY - 1, gy > 0
    going, coming = (has_next, has_last), (has_last, has_next)
    rows_near = has_next.astype(jnp.int32) + has_last.astype(jnp.int32)

    def signal(semaphore, device, condition=None):
        def act():
            pl.semaphore_signal(semaphore, inc=1, device_id=device, device_id_type=MESH)

        act() if condition is None else pl.when(condition)(act)

    barrier = pltpu.get_barrier_semaphore()
    for s in range(2):
        signal(barrier, near[s], going[s])
    signal(barrier, partner)
    signal(barrier, near[2], gx < NGX - 1)
    signal(barrier, near[3], gx == 0)
    greeted = (gx > 0).astype(jnp.int32) + (gx == NGX - 1).astype(jnp.int32)
    answered = (gx < NGX - 1).astype(jnp.int32) + (gx == 0).astype(jnp.int32)

    loads = [
        pltpu.make_async_copy(inc, imo.at[0:3, :, 0:16, :], load_sem.at[5]),
        pltpu.make_async_copy(mis, imo.at[3:6, :, 0:16, :], load_sem.at[6]),
    ]
    for f in range(VARS):
        loads.append(pltpu.make_async_copy(fine.at[f], fs.at[f], load_sem.at[f]))
    for f in range(2):
        loads.append(pltpu.make_async_copy(wind.at[f], wf.at[f], load_sem.at[3 + f]))
    for copy in loads:
        copy.start()

    source = lax.broadcasted_iota(jnp.int32, (FCOLS, 128), 0) // 4
    target = lax.broadcasted_iota(jnp.int32, (FCOLS, 128), 1)
    mean = jnp.where(source == target, 0.0625, 0.0).astype(BF16)
    table[0:FCOLS] = mean
    table[FCOLS : 2 * FCOLS] = mean

    started = []

    def when(condition, act):
        act() if condition is None else pl.when(condition)(act)

    def prepare(src, dst, device, goes=None, comes=None):
        i = len(started)
        copy = pltpu.make_async_remote_copy(
            src_ref=src, dst_ref=dst, send_sem=send_sem.at[i], recv_sem=recv_sem.at[i],
            device_id=device, device_id_type=MESH,
        )
        started.append((copy, goes))
        return copy, comes, goes

    def send(*args):
        message = prepare(*args)
        when(message[2], message[0].start)
        return message

    def start(message, condition):
        goes = message[2]
        both = condition if goes is None else jnp.logical_and(condition, goes)
        pl.when(both)(message[0].start)

    def arrive(message):
        when(message[1], message[0].wait_recv)

    def send_row(src, dst, s):
        return send(src, dst, near[s], going[s], coming[s])

    def relay(ref, at, comes=None):
        dst = ref.at[(*at, slice(16, 24), slice(None))]
        return send(ref.at[(*at, tile, slice(None))], dst, partner, comes, comes)

    tile = pl.ds(pl.multiple_of((1 - lev) * 8, 8), 8)
    lane = lax.broadcasted_iota(jnp.int32, (LEVS, 128), 1)

    def unit(f, j):
        if f < 5:
            return cwo[f, j, 0:16, :]
        body = imo[f - 5, j, 0:16, :]
        return jnp.concatenate([body, jnp.zeros((LEVS, 128 - COLS), F32)], axis=1)

    def row_of(s, k):
        return ROWS - k if s == 0 else k - 1

    def pack_rows(s, start, stop):
        for g in range(start // 3, stop // 3):
            parts = [unit(f, row_of(s, k)) for f, k in ITEMS[4 * g : 4 * g + 4]]
            for m in range(3):
                rest = pltpu.roll(parts[3], 96 - 32 * m, 1)
                ys[s, 3 * g + m] = jnp.where(lane < COLS, parts[m], rest)

    loads[0].wait()
    loads[1].wait()
    for s in range(2):
        pack_rows(s, 0, EARLY)
    def coarsen(f):
        loads[2 + f].wait()
        ref = fs[f] if f < VARS else wf[f - VARS]
        parts = jnp.concatenate(two_parts(ref.reshape(LEVS * FROWS, FCOLS)), axis=1)
        half[...] = jnp.dot(parts, table[...], preferred_element_type=F32)
        for j in range(ROWS):
            total = half[pl.ds(4 * j, LEVS, stride=FROWS), :]
            for a in range(1, 4):
                total += half[pl.ds(4 * j + a, LEVS, stride=FROWS), :]
            cwo[f, j, 0:16, :] = total

    coarsen(0)
    coarsen(1)
    pl.semaphore_wait(barrier, rows_near + greeted + 1)
    y_im = [send_row(ys.at[s, 0:EARLY], yp.at[s, 0:EARLY, 0:16, :], s) for s in range(2)]
    signal(answer, near[3], gx > 0)
    signal(answer, near[2], gx == NGX - 1)
    early, late = answered == 0, answered > 0
    between, lowest = jnp.logical_and(late, gx > 0), gx == 0
    signal(known, partner, early)
    own = [send(imo.at[:, :, tile, :], imo.at[:, :, 16:24, :], partner)]

    coarsen(2)
    pl.when(early)(lambda: pl.semaphore_wait(known, 1))
    for s in range(2):
        signal(ready, near[s], jnp.logical_and(going[s], early))
    coarsen(3)
    coarsen(4)
    def packed(out, value, h, at, width):
        first = COLS - width if h == 0 else 0
        moved = pltpu.roll(value, (at - first) % 128, 1)
        return jnp.where(jnp.logical_and(lane >= at, lane < at + width), moved, out)

    zero = jnp.zeros((LEVS, 128), F32)
    for h in range(2):
        for s in range(2):
            out = zero
            for (f, k), (at, width) in SEG_CORNER.items():
                out = packed(out, unit(f, row_of(s, k)), h, at, width)
            xs[h, 6 + s] = out
    def prepare_pair(h, at, device, goes=None, comes=None):
        there = xm.at[h, at]
        spread = (slice(None),) * (len(there.shape) - 2)
        low, adjacent = (*spread, slice(0, 16)), (*spread, slice(16, 24))
        cross = (*device[:2], 1 - lev)
        return [
            prepare(xs.at[h, at], there.at[low], device, goes, comes),
            prepare(xs.at[h, at].at[(*spread, tile)], there.at[adjacent], cross, goes, comes),
        ]

    corner = []
    for h in range(2):
        for s in range(2):
            device = (gxs[h], gys[s], lev)
            corner += prepare_pair(h, 6 + s, device, going[s], coming[s])

    def send_corners(condition):
        pl.when(condition)(lambda: pl.semaphore_wait(ready, rows_near))
        for message in corner:
            start(message, condition)

    send_corners(early)

    def hear(condition):
        pl.when(condition)(lambda: pl.semaphore_wait(answer, answered))
        signal(known, partner, condition)
        pl.when(condition)(lambda: pl.semaphore_wait(known, 1))
        for s in range(2):
            signal(ready, near[s], jnp.logical_and(going[s], condition))

    for s in range(2):
        pack_rows(s, EARLY, UNITS)
    y_cw = [
        send_row(ys.at[s, EARLY:UNITS], yp.at[s, EARLY:UNITS, 0:16, :], s) for s in range(2)
    ]
    own.append(send(cwo.at[:, :, tile, :], cwo.at[:, :, 16:24, :], partner))

    for h in range(2):
        for j in range(ROWS):
            out = zero
            for f, (at, width) in SEG_ROW.items():
                out = packed(out, unit(f, j), h, at, width)
            xs[h, j] = out
    x_row = []
    for h in range(2):
        x_row += prepare_pair(h, slice(0, 6), near[2 + h])
    hear(between)
    for message in x_row:
        start(message, gx > 0)
    edge = 15 * (1 - lev)
    fine_lev = send(fs.at[:, edge], fl, partner)

    for v in range(VARS):
        for l in range(LEVS):
            fys[0, v, l : l + 1, :] = fs[v, l, FROWS - 1 : FROWS, :]
            fys[1, v, l : l + 1, :] = fs[v, l, 0:1, :]
    y_fine = [
        prepare(fys.at[s], fy.at[s], near[s], going[s], coming[s]) for s in range(2)
    ]
    for message in y_fine:
        start(message, jnp.logical_or(early, lowest))

    lane8 = lax.broadcasted_iota(jnp.int32, (8, 128), 1)
    for v in range(VARS):
        outs = [jnp.zeros((8, 128), F32)] * 2
        for l in range(LEVS):
            for t in range(3):
                n = 3 * l + t
                first = pltpu.roll(fs[v, l, 8 * t : 8 * t + 8, 0:128], n, 1)
                last = pltpu.roll(fs[v, l, 8 * t : 8 * t + 8, 256:384], (n + 1) % 128, 1)
                outs[0] = jnp.where(lane8 == n, last, outs[0])
                outs[1] = jnp.where(lane8 == n, first, outs[1])
        fxs[0, v] = outs[0]
        fxs[1, v] = outs[1]
    x_fine = [prepare(fxs.at[h], fx.at[h], near[2 + h]) for h in range(2)]
    for message in x_fine:
        start(message, gx > 0)

    coarse_lane = lax.broadcasted_iota(jnp.int32, (128, FCOLS), 0)
    fine_col = lax.broadcasted_iota(jnp.int32, (128, FCOLS), 1)

    def columns(shift):
        scaled = 4 * (fine_col + shift) + 10
        beneath = lax.shift_right_arithmetic(scaled, 4)
        fraction = jnp.bitwise_and(scaled, 15).astype(F32) * 0.0625
        first = coarse_lane == jnp.bitwise_and(beneath - 1, 127)
        second = coarse_lane == jnp.bitwise_and(beneath, 127)
        return jnp.where(first, 1.0 - fraction, 0.0) + jnp.where(second, fraction, 0.0)

    middle = columns(0).astype(BF16)
    ahead, behind = columns(1), columns(-1)
    slant = (0.125 * (behind - ahead)).astype(BF16)
    around = (ahead + behind).astype(BF16)
    for part in range(2):
        rows = slice(128 * part, 128 * part + 128)
        table_a[rows, 0:FCOLS] = middle
        table_a[rows, FCOLS:] = slant
        table_b[rows, :] = middle
        table_b[slice(256 + 128 * part, 384 + 128 * part), :] = around

    row = lax.broadcasted_iota(jnp.int32, (FROWS, FCOLS), 0)
    col = lax.broadcasted_iota(jnp.int32, (FROWS, FCOLS), 1)

    def fine_step(l, carry):
        wu, wv = 0.125 * wf[0, l], 0.125 * wf[1, l]
        has_low = jnp.where(l > 0, 0.1, 0.0).astype(F32)
        has_high = jnp.where(l < LEVS - 1, 0.1, 0.0).astype(F32)
        for v in range(VARS):
            k = MIX[v]
            x = fs[v, l]
            total = (1.0 - 4.0 * k - 0.2) * x
            total += has_low * fs[v, jnp.maximum(l - 1, 0)]
            total += has_high * fs[v, jnp.minimum(l + 1, LEVS - 1)]
            total += (k - wu) * jnp.where(col == FCOLS - 1, 0.0, pltpu.roll(x, FCOLS - 1, 1))
            total += (k + wu) * jnp.where(col == 0, 0.0, pltpu.roll(x, 1, 1))
            total += (k - wv) * jnp.where(row == FROWS - 1, 0.0, pltpu.roll(x, FROWS - 1, 0))
            total += (k + wv) * jnp.where(row == 0, 0.0, pltpu.roll(x, 1, 0))
            base[v, l] = total
        return carry

    send_corners(between)
    for message in y_fine:
        start(message, between)
    lax.fori_loop(0, 10, fine_step, 0)
    hear(lowest)
    for message in x_row + x_fine:
        start(message, lowest)
    lax.fori_loop(10, LEVS, fine_step, 0)
    send_corners(lowest)

    relays = []
    for s in range(2):
        arrive(y_im[s])
        relays.append(relay(yp, (s, slice(0, EARLY)), coming[s]))
    for s in range(2):
        arrive(y_cw[s])
        relays.append(relay(yp, (s, slice(EARLY, UNITS)), coming[s]))
    for message in x_fine + [fine_lev]:
        arrive(message)

    def fine_columns(l, carry):
        for v in range(VARS):
            k = MIX[v]
            for t in range(3):
                n = 3 * l + t
                rows = slice(8 * t, 8 * t + 8)
                left = pltpu.roll(fx[0, v], lax.rem(128 - n, 128), 1)
                right = pltpu.roll(fx[1, v], 127 - n, 1)
                wu0, wu1 = 0.125 * wf[0, l, rows, 0:128], 0.125 * wf[0, l, rows, 256:384]
                base[v, l, rows, 0:128] += jnp.where(lane8 == 0, (k + wu0) * left, 0.0)
                base[v, l, rows, 256:384] += jnp.where(lane8 == 127, (k - wu1) * right, 0.0)
        return carry

    lax.fori_loop(0, LEVS, fine_columns, 0, unroll=2)
    for v in range(VARS):
        base[v, edge] += 0.1 * fl[v]

    for message in y_fine:
        arrive(message)
    sub8 = lax.broadcasted_iota(jnp.int32, (8, FCOLS), 0)

    def fine_rows(l, carry):
        for v in range(VARS):
            k = MIX[v]
            south = jnp.broadcast_to(fy[0, v, pl.ds(l, 1), :], (8, FCOLS))
            north = jnp.broadcast_to(fy[1, v, pl.ds(l, 1), :], (8, FCOLS))
            south = jnp.where(jnp.logical_and(sub8 == 0, gy > 0), south, 0.0)
            north = jnp.where(jnp.logical_and(sub8 == 7, gy < NGY - 1), north, 0.0)
            base[v, l, 0:8] += (k + 0.125 * wf[1, l, 0:8]) * south
            base[v, l, 16:24] += (k - 0.125 * wf[1, l, 16:24]) * north
        return carry

    lax.fori_loop(0, LEVS, fine_rows, 0, unroll=4)
    for message in own + relays + x_row + corner:
        arrive(message)
    for copy, goes in started:
        when(goes, copy.wait_send)


COPIES = 27


def exchange(fine, wind, inc, mis):
    return pl.pallas_call(
        exchange_kernel,
        out_shape=(
            pltpu.VMEM((VARS, LEVS, FROWS, FCOLS), F32),
            pltpu.VMEM((2, LEVS, FROWS, FCOLS), F32),
            pltpu.VMEM((VARS, LEVS, FROWS, FCOLS), F32),
            pltpu.VMEM((2, UNITS, 24, 128), F32),
            pltpu.VMEM((5, ROWS, 24, 128), F32),
            pltpu.VMEM((6, ROWS, 24, COLS), F32),
            pltpu.VMEM((2, 8, 24, 128), F32),
            pltpu.VMEM((256, 2 * FCOLS), BF16),
            pltpu.VMEM((512, FCOLS), BF16),
        ),
        in_specs=[HBM] * 4,
        out_specs=(VMEM,) * 9,
        scratch_shapes=[
            pltpu.VMEM((LEVS * FROWS, 128), F32),
            pltpu.VMEM((2, UNITS, LEVS, 128), F32),
            pltpu.VMEM((2, 8, LEVS, 128), F32),
            pltpu.VMEM((2, VARS, LEVS, FCOLS), F32),
            pltpu.VMEM((2, VARS, LEVS, FCOLS), F32),
            pltpu.VMEM((2, VARS, 8, 128), F32),
            pltpu.VMEM((2, VARS, 8, 128), F32),
            pltpu.VMEM((VARS, FROWS, FCOLS), F32),
            pltpu.VMEM((2 * FCOLS, 128), BF16),
            pltpu.SemaphoreType.DMA((7,)),
            pltpu.SemaphoreType.REGULAR,
            pltpu.SemaphoreType.REGULAR,
            pltpu.SemaphoreType.REGULAR,
            pltpu.SemaphoreType.DMA((COPIES,)),
            pltpu.SemaphoreType.DMA((COPIES,)),
        ],
        compiler_params=pltpu.CompilerParams(
            vmem_limit_bytes=20 << 20, collective_id=0, has_side_effects=True
        ),
        name="exchange",
    )(fine, wind, inc, mis)


def solve_kernel(
    fs, wf, base, yp, cwo, imo, xm, table_a, table_b,
    fine_next, gradient,
    q, st, sc, d1, res, a1, up, vr, lv, ly, grad, out, out_sem,
):
    gy, lev = lax.axis_index("gy"), lax.axis_index("lev")
    lane = lax.broadcasted_iota(jnp.int32, (24, 128), 1)
    level = lax.broadcasted_iota(jnp.int32, (24, 128), 0)
    top = jnp.where(lev == 1, 15, 24)
    bottom = jnp.where(lev == 0, 0, 24)
    above = jnp.where(level == top, 0.0, 0.1).astype(F32)
    below = jnp.where(level == bottom, 0.0, 0.1).astype(F32)

    first_row = jnp.where(gy == 0, 5, 0)
    last_row = jnp.where(gy == NGY - 1, 10, 15)

    def within(e):
        return jnp.logical_and(e >= first_row, e <= last_row)

    def inside(e):
        return jnp.where(within(e), 1.0, 0.0).astype(F32)

    def kept(value, e):
        return value if 5 <= e < 11 else value * inside(e)

    def fill(f, e, body, u, at, width):
        left = pltpu.roll(xm[0, u], (128 - width - at) % 128, 1)
        right = pltpu.roll(xm[1, u], (COLS - at) % 128, 1)
        value = jnp.where(lane < COLS, body, jnp.where(lane >= 112, left, right))
        if not 5 <= e < 11:
            value = jnp.where(within(e), value, 0.0)
        if f in (3, 4):
            value = 0.125 * value
        q[f, e] = value

    places = {}
    for s in range(2):
        for i, (f, k) in enumerate(ITEMS):
            places[f, 5 - k if s == 0 else 10 + k] = (s, i // 4, i % 4, k)

    def fill_row(fields, e):
        for f in fields:
            if 5 <= e < 11:
                if f < 5:
                    body = cwo[f, e - 5]
                else:
                    side = jnp.zeros((24, 128 - COLS), F32)
                    body = jnp.concatenate([imo[f - 5, e - 5], side], axis=1)
                fill(f, e, body, e - 5, *SEG_ROW[f])
            elif (f, e) in places:
                s, g, m, k = places[f, e]
                if m < 3:
                    body = yp[s, 3 * g + m]
                else:
                    third = [pltpu.roll(yp[s, 3 * g + n], 32 + 32 * n, 1) for n in range(3)]
                    body = jnp.where(lane < 32, third[0], jnp.where(lane < 64, third[1], third[2]))
                fill(f, e, body, 6 + s, *SEG_CORNER[f, k])

    def east(x):
        return pltpu.roll(x, 127, 1)

    def west(x):
        return pltpu.roll(x, 1, 1)

    def vertical(x):
        return pltpu.roll(x, 23, 0) * above + pltpu.roll(x, 1, 0) * below

    def adjoint(ref, v, e, wu, wn, ws):
        k = MIX[v]
        x = ref[v, e]
        total = (1.0 - 4.0 * k - 0.2) * x + vertical(x)
        total += east((k + wu) * x) + west((k - wu) * x)
        total += (k + wn) * ref[v, e + 1] + (k - ws) * ref[v, e - 1]
        return x, total

    def winds(e):
        return q[3, e], q[4, e]

    def weights(v, wu, wv):
        k = MIX[v]
        return k - wu, k + wu, k - wv, k + wv

    def centre(v, x):
        return (0.8 - 4.0 * MIX[v]) * x + vertical(x)

    def forward(ref, base, v, e, coefficients):
        to_east, to_west, to_north, to_south = coefficients
        x = ref[base + v, e]
        total = centre(v, x) + to_east * east(x) + to_west * west(x)
        total += to_north * ref[base + v, e + 1] + to_south * ref[base + v, e - 1]
        return x, total

    def stage_one(e, carry):
        wu, wv = winds(e)
        for v in range(VARS):
            coefficients = weights(v, wu, wv)
            t = jnp.tanh(q[v, e])
            s = 0.3 - 0.3 * t * t
            if 4 <= e < 12:
                sc[v, e] = s
            x, total = forward(q, 5, v, e, coefficients)
            d1[v, e] = kept(total - s * x, e)
            if 2 <= e < 14:
                _, total = forward(q, 0, v, e, coefficients)
                t = jnp.tanh(total - 0.3 * t)
                st[v, e] = 0.3 - 0.3 * t * t
        return carry


    def stage_two(e, carry):
        wu, wv = winds(e)
        for v in range(VARS):
            x, total = forward(d1, 0, v, e, weights(v, wu, wv))
            res[v, e] = kept(total - st[v, e] * x - q[8 + v, e], e)
        return carry


    def stage_three(e, carry):
        wu, _ = winds(e)
        wn, ws = q[4, e + 1], q[4, e - 1]
        for v in range(VARS):
            x, total = adjoint(res, v, e, wu, wn, ws)
            a1[v, e] = kept(total - st[v, e] * x, e)
        return carry


    def stage_four(e, carry):
        wu, _ = winds(e)
        wn, ws = q[4, e + 1], q[4, e - 1]
        for v in range(VARS):
            x, total = adjoint(a1, v, e, wu, wn, ws)
            start = q[5 + v, e]
            slant = start + total - sc[v, e] * x
            up[v, e - 4] = kept(start - 0.5 * slant, e)
            if 5 <= e < 11:
                grad[v, e - 5] = slant[0:16, 0:COLS]
        return carry

    for front in range(16 + 4):
        if front < 16:
            fill_row(range(8), front)
        e = front - 1
        if 1 <= e < 15:
            stage_one(e, 0)
        e = front - 2
        if 2 <= e < 14:
            fill_row(range(8, 11), e)
            stage_two(e, 0)
        e = front - 3
        if 3 <= e < 13:
            stage_three(e, 0)
        e = front - 4
        if 4 <= e < 12:
            stage_four(e, 0)

    grad_copy = pltpu.make_async_copy(grad, gradient, out_sem.at[6])
    grad_copy.start()

    pieces = ((0.375, 0.625, 0.0), (0.125, 0.875, 0.0), (0.0, 0.875, 0.125), (0.0, 0.625, 0.375))
    low, high = inside(4), inside(11)
    outs = []
    for v in range(VARS):
        k = MIX[v]
        rows = [up[v, e] for e in range(8)]

        def fine_row(r):
            j, a = r // 4, r % 4
            c = pieces[a]
            value = c[1] * rows[j + 1]
            value += c[0] * rows[j] if c[0] else c[2] * rows[j + 2]
            if r == -1:
                value = value * low
            if r == 24:
                value = value * high
            return value

        south, here = fine_row(-1), fine_row(0)
        for r in range(FROWS):
            north = fine_row(r + 1)
            mixed = ((0.8 - 4.0 * k) / k) * here + (north + south) + (1.0 / k) * vertical(here)
            at = pl.ds(24 * r, LEVS)
            vr[0, at, :] = here[0:16]
            vr[1, at, :] = mixed[0:16]
            vr[2, at, :] = 0.125 * (south - north)[0:16]
            south, here = here, north
        for l in range(0, LEVS, 2):
            at = pl.ds(24 * l, 48)

            def pair(i):
                one, two = vr[i, pl.ds(l, 24, stride=24), :], vr[i, pl.ds(l + 1, 24, stride=24), :]
                return two_parts(jnp.concatenate([one, two], axis=0))

            lv[at, 256:384], lv[at, 384:512] = pair(0)
            lv[at, 0:128], lv[at, 128:256] = pair(1)
            ly[at, 0:128], ly[at, 128:256] = pair(2)
        for c in range(2):
            at = slice(192 * c, 192 * c + 192)
            levels = slice(8 * c, 8 * c + 8)
            shape = (8, FROWS, FCOLS)

            def dot(x, t):
                return jnp.dot(x, t, preferred_element_type=F32).reshape(shape)

            both = jnp.dot(lv[at, 256:512], table_a[...], preferred_element_type=F32)
            step = both[:, 0:FCOLS].reshape(shape)
            total = base[v, levels] - 0.3 * jnp.tanh(fs[v, levels] + step)
            total += wf[0, levels] * both[:, FCOLS:].reshape(shape)
            total += k * dot(lv[at, :], table_b[...])
            total += wf[1, levels] * dot(ly[at, :], table_a[:, 0:FCOLS])
            out[v, levels] = total
            copy = pltpu.make_async_copy(
                out.at[v, levels], fine_next.at[v, levels], out_sem.at[2 * v + c]
            )
            copy.start()
            outs.append(copy)
    for copy in outs:
        copy.wait()
    grad_copy.wait()


def solve(*args):
    line = lambda n: pltpu.VMEM((n, 16, 24, 128), F32)
    return pl.pallas_call(
        solve_kernel,
        out_shape=(
            jax.ShapeDtypeStruct((VARS, LEVS, FROWS, FCOLS), F32),
            jax.ShapeDtypeStruct((VARS, ROWS, LEVS, COLS), F32),
        ),
        in_specs=[VMEM] * 9,
        out_specs=(HBM, HBM),
        scratch_shapes=[
            line(FIELDS), line(3), line(3), line(3), line(3), line(3),
            pltpu.VMEM((VARS, 8, 24, 128), F32),
            pltpu.VMEM((3, 24 * 24, 128), F32),
            pltpu.VMEM((LEVS * FROWS, 512), BF16),
            pltpu.VMEM((LEVS * FROWS, 256), BF16),
            pltpu.VMEM((VARS, ROWS, LEVS, COLS), F32),
            pltpu.VMEM((VARS, LEVS, FROWS, FCOLS), F32),
            pltpu.SemaphoreType.DMA((7,)),
        ],
        compiler_params=pltpu.CompilerParams(vmem_limit_bytes=40 << 20),
        name="solve",
    )(*args)


def per_device(fine_state, wind_field, increment, misfit):
    inc = jnp.transpose(increment, (0, 2, 1, 3))
    mis = jnp.transpose(misfit, (0, 2, 1, 3))
    held = [pltpu.with_memory_space_constraint(x, pltpu.HBM) for x in (fine_state, wind_field, inc, mis)]
    fine_next, gradient = solve(*exchange(*held))
    return fine_next, jnp.transpose(gradient, (0, 2, 1, 3))


def solution(mesh):
    spec = P(None, "lev", "gy", "gx")
    return jax.shard_map(
        per_device, mesh=mesh, in_specs=(spec,) * 4, out_specs=(spec, spec), check_vma=False
    )
```
